256 devices in a mesh: gx: 16 (over y_hi, z), gy: 16 (over y_lo, x, core).
Axes of the slice: x: 4, y: 4 (y_hi: 2, y_lo: 2; y = y_hi * 2 + y_lo), z: 8, core: 2. Of those that a mesh axis runs over, the one named last changes fastest.
Arguments:
- inputs: bfloat16 [32, 64, 48, 128], P('gx', 'gy'), may hold values from -6 to 6
- cotangent: bfloat16 [32, 64, 48, 128], P('gx', 'gy'), may hold values from -6 to 6
- kernel: bfloat16 [27, 128, 128], replicated, may hold values from -0.109375 to 0.109375
Outputs:
- input_grad: bfloat16 [32, 64, 48, 128], P('gx', 'gy')
- kernel_grad: float32 [27, 128, 128], P(None, 'gx', 'gy')
The draws below stay inside these ranges and needn't reach their ends.
All inputs are finite; a program needn't handle non-finite values.
Results may differ from the reference program's by a relative error of at most 0.0023.
Values may be sent and summed in bfloat16 or wider, within the bound.
A program may use at most 64 MiB of HBM per device.

```python
import math
import jax
import jax.numpy as jnp
from jax import lax

C = 128
DEPTH = 48
NX = 32
NY = 64


def raised(values, own_key, source, target, blocks, factor):
    owner, partner = [(jnp.arange(values.shape[dim]) // (values.shape[dim] // blocks)).reshape([-1 if axis == dim else 1 for axis in range(values.ndim)]) for dim in (source, target)]
    chosen = jax.random.permutation(own_key, blocks)[partner]
    strong = (owner == chosen) | (owner == (partner + blocks // 2) % blocks)
    return jnp.where(strong, factor * values, values)


def shard_levels(key, dims, shards, smallest, top_value):
    def one(axis_at, parts):
        heights = jax.random.uniform(jax.random.fold_in(jax.random.fold_in(key, 6), axis_at), (parts,), jnp.float32, smallest / len(shards), top_value / len(shards))
        return jnp.repeat(jnp.exp(heights), dims[axis_at] // parts).reshape((-1,) + (1,) * (len(dims) - axis_at - 1))

    loudness = one(*shards[0])
    for cut in shards[1:]:
        loudness = loudness * one(*cut)
    return loudness


def centred(stream_key, shape, width, reach, shards=(), held_as=jnp.bfloat16):
    values = width * jax.random.normal(stream_key, shape, jnp.float32)
    if shards:
        values = values * shard_levels(stream_key, shape, shards, -0.22, 0.18)
    return jnp.clip(values, -reach, reach).astype(held_as)


def heavy_noise(key, shape, spread, reach, cuts, heavy, kind=jnp.bfloat16):
    result = spread * jax.random.normal(key, shape, jnp.float32)
    if cuts:
        result = result * shard_levels(key, shape, cuts, -0.22, 0.18)
    return jnp.clip(raised(result, jax.random.fold_in(key, 3), *heavy), -reach, reach).astype(kind)


def setup_inputs(seed: int = 0) -> dict:
    key_list = jax.random.split(jax.random.key(seed), 4)
    return {
        "inputs": heavy_noise(key_list[0], (NX, NY, DEPTH, C), 1.0, 6.0, ((0, 16), (1, 16)), (1, 3, 16, 2.0)),
        "cotangent": heavy_noise(key_list[1], (NX, NY, DEPTH, C), 1.0, 6.0, ((0, 16), (1, 16)), (0, 3, 16, 2.0)),
        "kernel": centred(key_list[2], (27, C, C), (27 * C) ** -0.5, 0.109375),
    }


def reference(inputs, cotangent, kernel):
    widthx, widthy, depth, chans = inputs.shape
    values = inputs.astype(jnp.float32)
    act = (values * 0.5 * (1.0 + lax.erf(values / math.sqrt(2.0)))).astype(jnp.bfloat16)
    slope = 0.5 * (1.0 + lax.erf(values / math.sqrt(2.0))) + values * jnp.exp(-0.5 * values * values) / math.sqrt(2.0 * math.pi)
    act_pad = jnp.pad(act, ((1, 1), (1, 1), (1, 1), (0, 0)))
    cot_pad = jnp.pad(cotangent, ((1, 1), (1, 1), (1, 1), (0, 0)))
    cot_flat = cotangent.reshape(-1, chans)
    back = jnp.zeros((widthx * widthy * depth, chans), jnp.float32)
    grads = []
    for jx in range(3):
        for jy in range(3):
            for jz in range(3):
                tap = jx * 9 + jy * 3 + jz
                apiece = act_pad[jx:jx + widthx, jy:jy + widthy, jz:jz + depth].reshape(-1, chans)
                grads.append(jnp.dot(apiece.T, cot_flat, preferred_element_type=jnp.float32))
                gpiece = cot_pad[2 - jx:2 - jx + widthx, 2 - jy:2 - jy + widthy, 2 - jz:2 - jz + depth].reshape(-1, chans)
                back = back + jnp.dot(gpiece, kernel[tap].T, preferred_element_type=jnp.float32)
    input_grad = (slope * back.reshape(widthx, widthy, depth, chans)).astype(jnp.bfloat16)
    kernel_grad = jnp.stack(grads) / math.sqrt(widthx * widthy * depth)
    return (input_grad, kernel_grad)
```

```python
import math

import jax
import jax.numpy as jnp
from jax import lax
from jax.experimental import pallas as pl
from jax.experimental.pallas import tpu as pltpu
from jax.sharding import PartitionSpec as P

MESH = pl.DeviceIdType.MESH
F32 = jnp.float32
BF16 = jnp.bfloat16

WX, WY, DZ, C = 2, 4, 48, 128
VOX = WX * WY * DZ
NZ = 8
NQ = 8
NXY = 2 * NQ
PAIRS = 14
CHUNKS = (((0, 3), (0, 4)), ((3, 6), (4, 8)), ((6, 9), (8, 14)))
DIRS = tuple((dx, dy) for dx in (-1, 0, 1) for dy in (-1, 0, 1) if (dx, dy) != (0, 0))


def rim(d, width, send):
    if d == 0:
        return (1, width) if not send else (0, width)
    if send:
        return (width - 1, 1) if d > 0 else (0, 1)
    return (0, 1) if d > 0 else (width + 1, 1)


def body(
    inp_hbm, cot_hbm, ker_hbm, ig_ref, kg_ref,
    inp, wts, halo, stack, act_t, slope, acc, taps, parts, sib, xsend, xrecv, zsend, zrecv,
    load_sem, hsend_sem, hrecv_sem, ssend_sem, srecv_sem, xsend_sem, xrecv_sem, zsend_sem, zrecv_sem,
):
    gx, gy = lax.axis_index("gx"), lax.axis_index("gy")
    core, q = gy % 2, gy // 2
    z, yh = gx % NZ, gx // NZ
    here = yh * NQ + q
    other = gy + 1 - 2 * core

    def xy_peer(m):
        return ((m // NQ) * NZ + z, (m % NQ) * 2 + core)

    def z_peer(k):
        return (yh * NZ + k, gy)

    barrier = pltpu.get_barrier_semaphore()

    def greet(dev):
        pl.semaphore_signal(barrier, inc=1, device_id=dev, device_id_type=MESH)

    for dx, dy in DIRS:
        greet(((gx + dx + 16) % 16, (gy + dy + 16) % 16))
    greet((gx, other))

    @pl.loop(1, NXY)
    def _(d):
        greet(xy_peer((here + d) % NXY))

    @pl.loop(1, NZ)
    def _(d):
        greet(z_peer((z + d) % NZ))

    own = halo.at[pl.ds(1, WX), pl.ds(1, WY)]
    load_cot = pltpu.make_async_copy(cot_hbm, own, load_sem.at[0])
    load_inp = pltpu.make_async_copy(inp_hbm, inp, load_sem.at[1])
    load_ker = pltpu.make_async_copy(ker_hbm, wts, load_sem.at[2])
    load_cot.start()
    load_inp.start()
    load_ker.start()

    def has(d, at, size):
        if d == 0:
            return 1
        return jnp.where(at < size - 1, 1, 0) if d > 0 else jnp.where(at > 0, 1, 0)

    def hop(i):
        dx, dy = DIRS[i]
        sx, sy = rim(dx, WX, True), rim(dy, WY, True)
        lx, ly = rim(dx, WX, False), rim(dy, WY, False)
        return pltpu.make_async_remote_copy(
            src_ref=cot_hbm.at[pl.ds(*sx), pl.ds(*sy)],
            dst_ref=halo.at[pl.ds(*lx), pl.ds(*ly)],
            send_sem=hsend_sem.at[i],
            recv_sem=hrecv_sem.at[i],
            device_id=((gx + dx + 16) % 16, (gy + dy + 16) % 16),
            device_id_type=MESH,
        )

    pl.semaphore_wait(barrier, len(DIRS) + 1 + (NXY - 1) + (NZ - 1))

    for i, (dx, dy) in enumerate(DIRS):
        @pl.when(has(dx, gx, 16) * has(dy, gy, 16) == 1)
        def _():
            hop(i).start()

    for i, (dx, dy) in enumerate(DIRS):
        lx, ly = rim(dx, WX, False), rim(dy, WY, False)

        @pl.when(has(-dx, gx, 16) * has(-dy, gy, 16) == 0)
        def _():
            halo[pl.ds(*lx), pl.ds(*ly)] = jnp.zeros((lx[1], ly[1], DZ, C), BF16)

    load_inp.wait()

    @pl.loop(0, WX)
    def _(x):
        v = inp[x].astype(F32).reshape(WY * DZ, C)
        cdf = 0.5 * (1.0 + lax.erf(v / math.sqrt(2.0)))
        slope[x] = cdf + v * jnp.exp(-0.5 * v * v) / math.sqrt(2.0 * math.pi)
        act = (v * cdf).astype(BF16)
        act_t[x] = act.astype(F32).T.astype(BF16)

    row = lax.broadcasted_iota(jnp.int32, (DZ, C), 0)

    def restack(x, y):
        v = halo[x, y].astype(F32)
        up = jnp.where(row == DZ - 1, 0.0, pltpu.roll(v, DZ - 1, 0))
        down = jnp.where(row == 0, 0.0, pltpu.roll(v, 1, 0))
        stack[x, y] = jnp.concatenate([up, v, down], axis=1).astype(BF16)

    load_cot.wait()

    @pl.loop(0, WX * WY)
    def _(k):
        restack(1 + k // WY, 1 + k % WY)

    taps[27] = jnp.zeros((C, C), F32)
    load_ker.wait()

    for i, (dx, dy) in enumerate(DIRS):
        @pl.when(has(-dx, gx, 16) * has(-dy, gy, 16) == 1)
        def _():
            hop(i).wait_recv()

    @pl.loop(0, WY + 2)
    def _(y):
        restack(0, y)
        restack(WX + 1, y)

    @pl.loop(0, WX)
    def _(x):
        restack(1 + x, 0)
        restack(1 + x, WY + 1)

    def window(w):
        jx, jy = w // 3, w % 3
        return stack[pl.ds(2 - jx, WX), pl.ds(2 - jy, WY)].reshape(VOX, 3 * C)

    def sib_copy(k):
        lo, hi = CHUNKS[k][1]
        return pltpu.make_async_remote_copy(
            src_ref=parts.at[1 - core, pl.ds(lo, hi - lo)],
            dst_ref=sib.at[pl.ds(lo, hi - lo)],
            send_sem=ssend_sem.at[k],
            recv_sem=srecv_sem.at[k],
            device_id=(gx, other),
            device_id_type=MESH,
        )

    def xy_copy(k, d, arriving=False):
        lo, hi = CHUNKS[k][1][0] // 2, CHUNKS[k][1][1] // 2
        to = (here + d) % NXY
        slot = (here + NXY - d) % NXY if arriving else here
        return pltpu.make_async_remote_copy(
            src_ref=xsend.at[to, pl.ds(lo, hi - lo)],
            dst_ref=xrecv.at[slot, pl.ds(lo, hi - lo)],
            send_sem=xsend_sem.at[k, d],
            recv_sem=xrecv_sem.at[k, d],
            device_id=xy_peer(to),
            device_id_type=MESH,
        )

    def z_copy(d, arriving=False):
        to = (z + d) % NZ
        slot = (z + NZ - d) % NZ if arriving else z
        return pltpu.make_async_remote_copy(
            src_ref=zsend.at[to],
            dst_ref=zrecv.at[slot],
            send_sem=zsend_sem.at[d],
            recv_sem=zrecv_sem.at[d],
            device_id=z_peer(to),
            device_id_type=MESH,
        )

    lhs = jnp.concatenate([act_t[x] for x in range(WX)], axis=1)

    def compute(k):
        (w_lo, w_hi), (lo, hi) = CHUNKS[k]

        @pl.loop(w_lo, w_hi)
        def _(w):
            r = jnp.dot(lhs, window(w), preferred_element_type=F32)
            for jz in range(3):
                taps[3 * w + jz] = r[:, jz * C : (jz + 1) * C]

        @pl.loop(lo, hi)
        def _(u):
            for h in range(2):
                a = jnp.concatenate(
                    [taps[2 * u, 64 * h : 64 * h + 64], taps[2 * u + 1, 64 * h : 64 * h + 64]], axis=0
                )
                t = a.T.reshape(NQ, 2, 8, C)
                parts[0, u, h] = t[:, 0]
                parts[1, u, h] = t[:, 1]

        sib_copy(k).start()

    def forward(k):
        lo, hi = CHUNKS[k][1]
        sib_copy(k).wait_recv()

        @pl.loop(lo // 2, hi // 2)
        def _(v):
            for h in range(2):
                both = [parts[core, 2 * v + e, h] + sib[2 * v + e, h] for e in range(2)]
                xsend[NQ * h : NQ * h + NQ, v] = jnp.concatenate(both, axis=1).astype(BF16)

        @pl.loop(1, NXY)
        def _(d):
            xy_copy(k, d).start()

    compute(0)
    compute(1)
    forward(0)
    compute(2)
    forward(1)
    forward(2)

    acc[...] = jnp.zeros_like(acc)

    @pl.loop(0, 9)
    def _(w):
        wt = jnp.concatenate([wts[3 * w + jz] for jz in range(3)], axis=1)
        acc[...] += lax.dot_general(
            window(w), wt, (((1,), (1,)), ((), ())), preferred_element_type=F32
        )

    for x in range(WX):
        back = acc[pl.ds(x * WY * DZ, WY * DZ)]
        ig_ref[x] = (slope[x] * back).astype(BF16).reshape(WY, DZ, C)

    for k in range(len(CHUNKS)):
        @pl.loop(1, NXY)
        def _(d):
            xy_copy(k, d, arriving=True).wait_recv()

    xrecv[here] = xsend[here]
    total = xrecv[0].astype(F32)
    for m in range(1, NXY):
        total = total + xrecv[m].astype(F32)
    total = jnp.concatenate([total.reshape(8 * PAIRS, C), jnp.zeros((C - 8 * PAIRS, C), F32)], axis=0)
    turned = total.T.reshape(2, NZ, 8, C)
    for e in range(2):
        zsend[:, e] = turned[e]

    @pl.loop(1, NZ)
    def _(d):
        z_copy(d).start()

    zrecv[z] = zsend[z]

    @pl.loop(1, NZ)
    def _(d):
        z_copy(d, arriving=True).wait_recv()

    out = zrecv[0]
    for m in range(1, NZ):
        out = out + zrecv[m]
    kg_ref[...] = out

    for i, (dx, dy) in enumerate(DIRS):
        @pl.when(has(dx, gx, 16) * has(dy, gy, 16) == 1)
        def _():
            hop(i).wait_send()

    for k in range(len(CHUNKS)):
        sib_copy(k).wait_send()

        @pl.loop(1, NXY)
        def _(d):
            xy_copy(k, d).wait_send()

    @pl.loop(1, NZ)
    def _(d):
        z_copy(d).wait_send()


def local(inputs, cotangent, kernel):
    n = len(CHUNKS)
    hbm = pl.BlockSpec(memory_space=pl.ANY)
    vmem = pl.BlockSpec(memory_space=pltpu.VMEM)
    dma = pltpu.SemaphoreType.DMA
    input_grad, sums = pl.pallas_call(
        body,
        out_shape=(
            jax.ShapeDtypeStruct((WX, WY, DZ, C), BF16),
            jax.ShapeDtypeStruct((2, 8, C), F32),
        ),
        in_specs=[hbm, hbm, hbm],
        out_specs=(vmem, vmem),
        scratch_shapes=[
            pltpu.VMEM((WX, WY, DZ, C), BF16),
            pltpu.VMEM((27, C, C), BF16),
            pltpu.VMEM((WX + 2, WY + 2, DZ, C), BF16),
            pltpu.VMEM((WX + 2, WY + 2, DZ, 3 * C), BF16),
            pltpu.VMEM((WX, C, WY * DZ), BF16),
            pltpu.VMEM((WX, WY * DZ, C), F32),
            pltpu.VMEM((VOX, C), F32),
            pltpu.VMEM((28, C, C), F32),
            pltpu.VMEM((2, PAIRS, 2, NQ, 8, C), F32),
            pltpu.VMEM((PAIRS, 2, NQ, 8, C), F32),
            pltpu.VMEM((NXY, PAIRS // 2, 16, C), BF16),
            pltpu.VMEM((NXY, PAIRS // 2, 16, C), BF16),
            pltpu.VMEM((NZ, 2, 8, C), F32),
            pltpu.VMEM((NZ, 2, 8, C), F32),
            dma((3,)),
            dma((8,)),
            dma((8,)),
            dma((n,)),
            dma((n,)),
            dma((n, NXY)),
            dma((n, NXY)),
            dma((NZ,)),
            dma((NZ,)),
        ],
        compiler_params=pltpu.CompilerParams(
            collective_id=0, has_side_effects=True, vmem_limit_bytes=32 * 1024 * 1024
        ),
        name="conv_backward",
    )(*(pltpu.with_memory_space_constraint(a, pltpu.HBM) for a in (inputs, cotangent, kernel)))
    voxels = 32 * 64 * 48
    grad = sums.reshape(2, 8, 16, 8).transpose(2, 0, 1, 3).reshape(32, 8, 8)[:27]
    return (input_grad, grad / math.sqrt(voxels))


def solution(mesh):
    return jax.shard_map(
        local,
        mesh=mesh,
        in_specs=(P("gx", "gy", None, None), P("gx", "gy", None, None), P()),
        out_specs=(P("gx", "gy", None, None), P(None, "gx", "gy")),
        check_vma=False,
    )
```

```python
import math

import jax
import jax.numpy as jnp
from jax import lax
from jax.experimental import pallas as pl
from jax.experimental.pallas import tpu as pltpu
from jax.sharding import PartitionSpec as P

MESH = pl.DeviceIdType.MESH
F32 = jnp.float32
BF16 = jnp.bfloat16

WX, WY, DZ, C = 2, 4, 48, 128
VOX = WX * WY * DZ
NZ = 8
NQ = 8
NXY = 2 * NQ
PAIRS = 14
ORDER = (3, 4, 5, 0, 1, 2, 6, 7, 8)
CHUNKS = (((0, 3), (0, 4)), ((3, 6), (4, 8)), ((6, 9), (8, 14)))
DIRS = tuple((dx, dy) for dx in (-1, 0, 1) for dy in (-1, 0, 1) if (dx, dy) != (0, 0))


def blocks(w, local):
    jx, jy = w // 3, w % 3
    every = [(x, y) for x in range(WX) for y in range(WY)]
    inside = [(x, y) for x, y in every if 1 <= x + 2 - jx <= WX and 1 <= y + 2 - jy <= WY]
    return inside if local else [b for b in every if b not in inside]


LOCAL = [blocks(w, True) for w in range(9)]
RIM = [blocks(w, False) for w in range(9)]


def rim(d, width, send):
    if d == 0:
        return (1, width) if not send else (0, width)
    if send:
        return (width - 1, 1) if d > 0 else (0, 1)
    return (0, 1) if d > 0 else (width + 1, 1)


def body(
    inp_hbm, cot_hbm, ker_hbm, ig_ref, kg_ref,
    inp, wts, halo, stack, act, slope, acc, taps, parts, sib, xsend, xrecv, zsend, zrecv, sums,
    load_sem, hsend_sem, hrecv_sem, ssend_sem, srecv_sem, xsend_sem, xrecv_sem, zsend_sem, zrecv_sem,
):
    gx, gy = lax.axis_index("gx"), lax.axis_index("gy")
    core, q = gy % 2, gy // 2
    z, yh = gx % NZ, gx // NZ
    here = yh * NQ + q
    other = gy + 1 - 2 * core

    def xy_peer(m):
        return ((m // NQ) * NZ + z, (m % NQ) * 2 + core)

    def z_peer(k):
        return (yh * NZ + k, gy)

    barrier = pltpu.get_barrier_semaphore()

    def greet(dev):
        pl.semaphore_signal(barrier, inc=1, device_id=dev, device_id_type=MESH)

    for dx, dy in DIRS:
        greet(((gx + dx + 16) % 16, (gy + dy + 16) % 16))
    greet((gx, other))

    @pl.loop(1, NXY)
    def _(d):
        greet(xy_peer((here + d) % NXY))

    @pl.loop(1, NZ)
    def _(d):
        greet(z_peer((z + d) % NZ))

    own = halo.at[pl.ds(1, WX), pl.ds(1, WY)]
    load_cot = pltpu.make_async_copy(cot_hbm, own, load_sem.at[0])
    load_inp = pltpu.make_async_copy(inp_hbm, inp, load_sem.at[1])
    load_ker = pltpu.make_async_copy(ker_hbm, wts, load_sem.at[2])
    load_cot.start()
    load_inp.start()
    load_ker.start()

    def has(d, at, size):
        if d == 0:
            return 1
        return jnp.where(at < size - 1, 1, 0) if d > 0 else jnp.where(at > 0, 1, 0)

    def hop(i):
        dx, dy = DIRS[i]
        sx, sy = rim(dx, WX, True), rim(dy, WY, True)
        lx, ly = rim(dx, WX, False), rim(dy, WY, False)
        return pltpu.make_async_remote_copy(
            src_ref=cot_hbm.at[pl.ds(*sx), pl.ds(*sy)],
            dst_ref=halo.at[pl.ds(*lx), pl.ds(*ly)],
            send_sem=hsend_sem.at[i],
            recv_sem=hrecv_sem.at[i],
            device_id=((gx + dx + 16) % 16, (gy + dy + 16) % 16),
            device_id_type=MESH,
        )

    pl.semaphore_wait(barrier, len(DIRS) + 1 + (NXY - 1) + (NZ - 1))

    for i, (dx, dy) in enumerate(DIRS):
        @pl.when(has(dx, gx, 16) * has(dy, gy, 16) == 1)
        def _():
            hop(i).start()

    for i, (dx, dy) in enumerate(DIRS):
        lx, ly = rim(dx, WX, False), rim(dy, WY, False)

        @pl.when(has(-dx, gx, 16) * has(-dy, gy, 16) == 0)
        def _():
            halo[pl.ds(*lx), pl.ds(*ly)] = jnp.zeros((lx[1], ly[1], DZ, C), BF16)

    load_inp.wait()

    @pl.loop(0, WX)
    def _(x):
        v = inp[x].astype(F32).reshape(WY * DZ, C)
        cdf = 0.5 * (1.0 + lax.erf(v / math.sqrt(2.0)))
        slope[x] = cdf + v * jnp.exp(-0.5 * v * v) / math.sqrt(2.0 * math.pi)
        act[x] = (v * cdf).astype(BF16).astype(F32).reshape(WY, DZ, C)

    row = lax.broadcasted_iota(jnp.int32, (DZ, C), 0)

    def restack(x, y):
        v = halo[x, y].astype(F32)
        up = jnp.where(row == DZ - 1, 0.0, pltpu.roll(v, DZ - 1, 0))
        down = jnp.where(row == 0, 0.0, pltpu.roll(v, 1, 0))
        stack[x, y] = jnp.concatenate([up, v, down], axis=1).astype(BF16)

    load_cot.wait()

    @pl.loop(0, WX * WY)
    def _(k):
        restack(1 + k // WY, 1 + k % WY)

    def gather(lhs_blocks):
        return jnp.concatenate([act[x, y] for x, y in lhs_blocks], axis=0).T.astype(BF16)

    def product(w, chosen):
        jx, jy = w // 3, w % 3
        rows = [stack[x + 2 - jx, y + 2 - jy] for x, y in chosen]
        return jnp.dot(lhs[w, chosen is RIM[w]], jnp.concatenate(rows, axis=0), preferred_element_type=F32)

    lhs = {}
    for w in ORDER:
        lhs[w, False] = gather(LOCAL[w])
        if RIM[w]:
            lhs[w, True] = gather(RIM[w])
    for n, w in enumerate(ORDER):
        r = product(w, LOCAL[w])
        for jz in range(3):
            taps[3 * n + jz] = r[:, jz * C : (jz + 1) * C]
    taps[27] = jnp.zeros((C, C), F32)
    load_ker.wait()

    def landed(along_x):
        for i, (dx, dy) in enumerate(DIRS):
            if (dx != 0) != along_x:
                continue

            @pl.when(has(-dx, gx, 16) * has(-dy, gy, 16) == 1)
            def _():
                hop(i).wait_recv()

    def window(w):
        jx, jy = w // 3, w % 3
        return stack[pl.ds(2 - jx, WX), pl.ds(2 - jy, WY)].reshape(VOX, 3 * C)

    def sib_copy(k):
        lo, hi = CHUNKS[k][1]
        return pltpu.make_async_remote_copy(
            src_ref=parts.at[1 - core, pl.ds(lo, hi - lo)],
            dst_ref=sib.at[pl.ds(lo, hi - lo)],
            send_sem=ssend_sem.at[k],
            recv_sem=srecv_sem.at[k],
            device_id=(gx, other),
            device_id_type=MESH,
        )

    def xy_copy(k, d, arriving=False):
        lo, hi = CHUNKS[k][1][0] // 2, CHUNKS[k][1][1] // 2
        to = (here + d) % NXY
        slot = (here + NXY - d) % NXY if arriving else here
        return pltpu.make_async_remote_copy(
            src_ref=xsend.at[to, pl.ds(lo, hi - lo)],
            dst_ref=xrecv.at[slot, pl.ds(lo, hi - lo)],
            send_sem=xsend_sem.at[k, d],
            recv_sem=xrecv_sem.at[k, d],
            device_id=xy_peer(to),
            device_id_type=MESH,
        )

    def z_copy(d, arriving=False):
        to = (z + d) % NZ
        slot = (z + NZ - d) % NZ if arriving else z
        return pltpu.make_async_remote_copy(
            src_ref=zsend.at[to],
            dst_ref=zrecv.at[slot],
            send_sem=zsend_sem.at[d],
            recv_sem=zrecv_sem.at[d],
            device_id=z_peer(to),
            device_id_type=MESH,
        )

    def compute(k):
        (w_lo, w_hi), (lo, hi) = CHUNKS[k]
        for n in range(w_lo, w_hi):
            w = ORDER[n]
            if RIM[w]:
                r = product(w, RIM[w])
                for jz in range(3):
                    taps[3 * n + jz] += r[:, jz * C : (jz + 1) * C]

        @pl.loop(lo, hi)
        def _(u):
            for h in range(2):
                a = jnp.concatenate(
                    [taps[2 * u, 64 * h : 64 * h + 64], taps[2 * u + 1, 64 * h : 64 * h + 64]], axis=0
                )
                t = a.T.reshape(NQ, 2, 8, C)
                parts[0, u, h] = t[:, 0]
                parts[1, u, h] = t[:, 1]

        sib_copy(k).start()

    def forward(k):
        lo, hi = CHUNKS[k][1]
        sib_copy(k).wait_recv()

        @pl.loop(lo // 2, hi // 2)
        def _(v):
            for h in range(2):
                both = [parts[core, 2 * v + e, h] + sib[2 * v + e, h] for e in range(2)]
                xsend[NQ * h : NQ * h + NQ, v] = jnp.concatenate(both, axis=1).astype(BF16)

        @pl.loop(1, NXY)
        def _(d):
            xy_copy(k, d).start()

    landed(False)

    @pl.loop(0, WX)
    def _(x):
        restack(1 + x, 0)
        restack(1 + x, WY + 1)

    compute(0)
    landed(True)

    @pl.loop(0, WY + 2)
    def _(y):
        restack(0, y)
        restack(WX + 1, y)

    compute(1)
    forward(0)
    compute(2)
    forward(1)
    forward(2)

    acc[...] = jnp.zeros_like(acc)

    @pl.loop(0, 9)
    def _(w):
        wt = jnp.concatenate([wts[3 * w + jz] for jz in range(3)], axis=1)
        acc[...] += lax.dot_general(
            window(w), wt, (((1,), (1,)), ((), ())), preferred_element_type=F32
        )

    for x in range(WX):
        back = acc[pl.ds(x * WY * DZ, WY * DZ)]
        ig_ref[x] = (slope[x] * back).astype(BF16).reshape(WY, DZ, C)

    for k in range(len(CHUNKS)):
        @pl.loop(1, NXY)
        def _(d):
            xy_copy(k, d, arriving=True).wait_recv()

    xrecv[here] = xsend[here]
    total = xrecv[0].astype(F32)
    for m in range(1, NXY):
        total = total + xrecv[m].astype(F32)
    sums[pl.ds(0, 8 * PAIRS)] = total.reshape(8 * PAIRS, C)
    sums[pl.ds(8 * PAIRS, C - 8 * PAIRS)] = jnp.zeros((C - 8 * PAIRS, C), F32)
    total = jnp.concatenate([sums[pl.ds(o, 16, stride=8)] for o in range(8)], axis=0)
    turned = total.T.reshape(2, NZ, 8, C)
    for e in range(2):
        zsend[:, e] = turned[e]

    @pl.loop(1, NZ)
    def _(d):
        z_copy(d).start()

    zrecv[z] = zsend[z]

    @pl.loop(1, NZ)
    def _(d):
        z_copy(d, arriving=True).wait_recv()

    out = zrecv[0]
    for m in range(1, NZ):
        out = out + zrecv[m]
    kg_ref[...] = out

    for i, (dx, dy) in enumerate(DIRS):
        @pl.when(has(dx, gx, 16) * has(dy, gy, 16) == 1)
        def _():
            hop(i).wait_send()

    for k in range(len(CHUNKS)):
        sib_copy(k).wait_send()

        @pl.loop(1, NXY)
        def _(d):
            xy_copy(k, d).wait_send()

    @pl.loop(1, NZ)
    def _(d):
        z_copy(d).wait_send()


def finish(ig_ref, sums_ref, out_ref, grad_ref, turn):
    out_ref[...] = ig_ref[...]
    total = sums_ref[...].reshape(16, C) / math.sqrt(32 * 64 * 48)
    for o in range(8):
        turn[pl.ds(o, 16, stride=8)] = pltpu.roll(total, (C - 16 * o) % C, 1)
    pair = turn[...].reshape(2, 8, 8, C)
    lane = lax.broadcasted_iota(jnp.int32, (8, C), 1)
    block = lane // 9
    place = lane + jnp.where(block == 0, 9, jnp.where(block == 1, -9, 0))
    source = jnp.minimum(place // 2, 15)
    for i in range(8):
        even = jnp.take_along_axis(pair[0, i], source, axis=1)
        odd = jnp.take_along_axis(pair[1, i], source, axis=1)
        grad_ref[i] = jnp.where(place % 2 == 0, even, odd)[:, :27]


def local(inputs, cotangent, kernel):
    n = len(CHUNKS)
    hbm = pl.BlockSpec(memory_space=pl.ANY)
    vmem = pl.BlockSpec(memory_space=pltpu.VMEM)
    dma = pltpu.SemaphoreType.DMA
    input_grad, sums = pl.pallas_call(
        body,
        out_shape=(
            jax.ShapeDtypeStruct((WX, WY, DZ, C), BF16),
            jax.ShapeDtypeStruct((2, 8, C), F32),
        ),
        in_specs=[hbm, hbm, hbm],
        out_specs=(vmem, vmem),
        scratch_shapes=[
            pltpu.VMEM((WX, WY, DZ, C), BF16),
            pltpu.VMEM((27, C, C), BF16),
            pltpu.VMEM((WX + 2, WY + 2, DZ, C), BF16),
            pltpu.VMEM((WX + 2, WY + 2, DZ, 3 * C), BF16),
            pltpu.VMEM((WX, WY, DZ, C), F32),
            pltpu.VMEM((WX, WY * DZ, C), F32),
            pltpu.VMEM((VOX, C), F32),
            pltpu.VMEM((28, C, C), F32),
            pltpu.VMEM((2, PAIRS, 2, NQ, 8, C), F32),
            pltpu.VMEM((PAIRS, 2, NQ, 8, C), F32),
            pltpu.VMEM((NXY, PAIRS // 2, 16, C), BF16),
            pltpu.VMEM((NXY, PAIRS // 2, 16, C), BF16),
            pltpu.VMEM((NZ, 2, 8, C), F32),
            pltpu.VMEM((NZ, 2, 8, C), F32),
            pltpu.VMEM((C, C), F32),
            dma((3,)),
            dma((8,)),
            dma((8,)),
            dma((n,)),
            dma((n,)),
            dma((n, NXY)),
            dma((n, NXY)),
            dma((NZ,)),
            dma((NZ,)),
        ],
        compiler_params=pltpu.CompilerParams(
            collective_id=0, has_side_effects=True, vmem_limit_bytes=32 * 1024 * 1024
        ),
        name="conv_backward",
    )(*(pltpu.with_memory_space_constraint(a, pltpu.HBM) for a in (inputs, cotangent, kernel)))
    whole = lambda shape: pl.BlockSpec(shape, lambda: (0,) * len(shape))
    input_grad, grad = pl.pallas_call(
        finish,
        out_shape=(
            jax.ShapeDtypeStruct((WX, WY, DZ, C), BF16),
            jax.ShapeDtypeStruct((8, 8, 27), F32),
        ),
        in_specs=[vmem, vmem],
        out_specs=(whole((WX, WY, DZ, C)), whole((8, 8, 27))),
        scratch_shapes=[pltpu.VMEM((C, C), F32)],
        compiler_params=pltpu.CompilerParams(vmem_limit_bytes=2 * 1024 * 1024),
        name="finish",
    )(input_grad, sums)
    return (input_grad, grad.transpose(2, 0, 1))


def solution(mesh):
    return jax.shard_map(
        local,
        mesh=mesh,
        in_specs=(P("gx", "gy", None, None), P("gx", "gy", None, None), P()),
        out_specs=(P("gx", "gy", None, None), P(None, "gx", "gy")),
        check_vma=False,
    )
```

```python
import math

import jax
import jax.numpy as jnp
from jax import lax
from jax.experimental import pallas as pl
from jax.experimental.pallas import tpu as pltpu
from jax.sharding import PartitionSpec as P

MESH = pl.DeviceIdType.MESH
F32 = jnp.float32
BF16 = jnp.bfloat16

WX, WY, DZ, C = 2, 4, 48, 128
VOX = WX * WY * DZ
NZ = 8
NQ = 8
NXY = 2 * NQ
PAIRS = 14
ORDER = (4, 3, 5, 0, 1, 2, 6, 7, 8)
CHUNKS = (((0, 1), (0, 1)), ((1, 3), (1, 2)), ((3, 6), (2, 4)), ((6, 9), (4, 7)))
STEPS = ('c0', 'f0', 'y', 'c1', 'x', 'c2', 'f1', 'c3', 'f2', 'f3')


def slot(n, jz):
    return 3 * n + jz + (1 if n else 0)


XY = sorted(
    ((dx, dy) for dx in range(4) for dy in range(4) if dx or dy),
    key=lambda d: -(min(d[0], 4 - d[0]) + min(d[1], 4 - d[1])),
)
ZS = (4, 3, 5, 2, 6, 1, 7)
DIRS = tuple((dx, dy) for dx in (-1, 0, 1) for dy in (-1, 0, 1) if (dx, dy) != (0, 0))


def blocks(w, local):
    jx, jy = w // 3, w % 3
    every = [(x, y) for x in range(WX) for y in range(WY)]
    inside = [(x, y) for x, y in every if 1 <= x + 2 - jx <= WX and 1 <= y + 2 - jy <= WY]
    return inside if local else [b for b in every if b not in inside]


LOCAL = [blocks(w, True) for w in range(9)]
RIM = [blocks(w, False) for w in range(9)]


def rim(d, width, send):
    if d == 0:
        return (1, width) if not send else (0, width)
    if send:
        return (width - 1, 1) if d > 0 else (0, 1)
    return (0, 1) if d > 0 else (width + 1, 1)


def body(
    inp_hbm, cot_hbm, ker_hbm, ig_ref, kg_ref,
    inp, wts, halo, stack, act, slope, acc, taps, parts, sib, xsend, xrecv, zsend, zrecv, sums,
    load_sem, hsend_sem, hrecv_sem, ssend_sem, srecv_sem, xsend_sem, xrecv_sem, zsend_sem, zrecv_sem,
):
    gx, gy = lax.axis_index("gx"), lax.axis_index("gy")
    core, q = gy % 2, gy // 2
    z, yh = gx % NZ, gx // NZ
    here = yh * NQ + q
    px, py = q % 4, yh * 2 + q // 4
    other = gy + 1 - 2 * core

    def xy_peer(d):
        x, y = (px + d[0]) % 4, (py + d[1]) % 4
        m = y * 4 + x
        return m, ((m // NQ) * NZ + z, (m % NQ) * 2 + core)

    def z_peer(k):
        return (yh * NZ + k, gy)

    barrier = pltpu.get_barrier_semaphore()

    def greet(dev):
        pl.semaphore_signal(barrier, inc=1, device_id=dev, device_id_type=MESH)

    for d in XY:
        greet(xy_peer(d)[1])
    for d in ZS:
        greet(z_peer((z + d) % NZ))
    for dx, dy in DIRS:
        greet(((gx + dx + 16) % 16, (gy + dy + 16) % 16))
    greet((gx, other))

    own = halo.at[pl.ds(1, WX), pl.ds(1, WY)]
    load_cot = pltpu.make_async_copy(cot_hbm, own, load_sem.at[0])
    load_inp = pltpu.make_async_copy(inp_hbm, inp, load_sem.at[1])
    load_ker = pltpu.make_async_copy(ker_hbm, wts, load_sem.at[2])
    load_cot.start()
    load_inp.start()
    load_ker.start()

    def has(d, at, size):
        if d == 0:
            return 1
        return jnp.where(at < size - 1, 1, 0) if d > 0 else jnp.where(at > 0, 1, 0)

    def hop(i):
        dx, dy = DIRS[i]
        sx, sy = rim(dx, WX, True), rim(dy, WY, True)
        lx, ly = rim(dx, WX, False), rim(dy, WY, False)
        return pltpu.make_async_remote_copy(
            src_ref=cot_hbm.at[pl.ds(*sx), pl.ds(*sy)],
            dst_ref=halo.at[pl.ds(*lx), pl.ds(*ly)],
            send_sem=hsend_sem.at[i],
            recv_sem=hrecv_sem.at[i],
            device_id=((gx + dx + 16) % 16, (gy + dy + 16) % 16),
            device_id_type=MESH,
        )

    pl.semaphore_wait(barrier, len(DIRS) + 1 + (NXY - 1) + (NZ - 1))

    for i, (dx, dy) in enumerate(DIRS):
        @pl.when(has(dx, gx, 16) * has(dy, gy, 16) == 1)
        def _():
            hop(i).start()

    for i, (dx, dy) in enumerate(DIRS):
        lx, ly = rim(dx, WX, False), rim(dy, WY, False)

        @pl.when(has(-dx, gx, 16) * has(-dy, gy, 16) == 0)
        def _():
            halo[pl.ds(*lx), pl.ds(*ly)] = jnp.zeros((lx[1], ly[1], DZ, C), BF16)

    load_inp.wait()

    @pl.loop(0, WX)
    def _(x):
        v = inp[x].astype(F32).reshape(WY * DZ, C)
        cdf = 0.5 * (1.0 + lax.erf(v / math.sqrt(2.0)))
        slope[x] = cdf + v * jnp.exp(-0.5 * v * v) / math.sqrt(2.0 * math.pi)
        act[x] = (v * cdf).astype(BF16).astype(F32).reshape(WY, DZ, C)

    row = lax.broadcasted_iota(jnp.int32, (DZ, C), 0)

    def restack(x, y):
        v = halo[x, y].astype(F32)
        up = jnp.where(row == DZ - 1, 0.0, pltpu.roll(v, DZ - 1, 0))
        down = jnp.where(row == 0, 0.0, pltpu.roll(v, 1, 0))
        stack[x, y] = jnp.concatenate([up, v, down], axis=1).astype(BF16)

    load_cot.wait()

    @pl.loop(0, WX * WY)
    def _(k):
        restack(1 + k // WY, 1 + k % WY)

    def gather(lhs_blocks):
        return jnp.concatenate([act[x, y] for x, y in lhs_blocks], axis=0).T.astype(BF16)

    def product(w, chosen):
        jx, jy = w // 3, w % 3
        rows = [stack[x + 2 - jx, y + 2 - jy] for x, y in chosen]
        return jnp.dot(lhs[w, chosen is RIM[w]], jnp.concatenate(rows, axis=0), preferred_element_type=F32)

    lhs = {}
    for w in ORDER:
        lhs[w, False] = gather(LOCAL[w])
        if RIM[w]:
            lhs[w, True] = gather(RIM[w])
    for n, w in enumerate(ORDER):
        r = product(w, LOCAL[w])
        for jz in range(3):
            taps[slot(n, jz)] = r[:, jz * C : (jz + 1) * C]
    taps[3] = jnp.zeros((C, C), F32)
    def landed(along_x):
        for i, (dx, dy) in enumerate(DIRS):
            if (dx != 0) != along_x:
                continue

            @pl.when(has(-dx, gx, 16) * has(-dy, gy, 16) == 1)
            def _():
                hop(i).wait_recv()

    def window(w):
        jx, jy = w // 3, w % 3
        return stack[pl.ds(2 - jx, WX), pl.ds(2 - jy, WY)].reshape(VOX, 3 * C)

    def sib_copy(k):
        lo, hi = CHUNKS[k][1]
        return pltpu.make_async_remote_copy(
            src_ref=parts.at[1 - core, pl.ds(2 * lo, 2 * (hi - lo))],
            dst_ref=sib.at[pl.ds(2 * lo, 2 * (hi - lo))],
            send_sem=ssend_sem.at[k],
            recv_sem=srecv_sem.at[k],
            device_id=(gx, other),
            device_id_type=MESH,
        )

    def xy_copy(k, d):
        lo, hi = CHUNKS[k][1]
        m, twin = xy_peer(d)
        return pltpu.make_async_remote_copy(
            src_ref=xsend.at[m, pl.ds(lo, hi - lo)],
            dst_ref=xrecv.at[here, pl.ds(lo, hi - lo)],
            send_sem=xsend_sem.at[k],
            recv_sem=xrecv_sem.at[k],
            device_id=twin,
            device_id_type=MESH,
        )

    def xy_all(k):
        lo, hi = CHUNKS[k][1]
        return pltpu.make_async_remote_copy(
            src_ref=xsend.at[pl.ds(0, NXY - 1), pl.ds(lo, hi - lo)],
            dst_ref=xrecv.at[pl.ds(0, NXY - 1), pl.ds(lo, hi - lo)],
            send_sem=xsend_sem.at[k],
            recv_sem=xrecv_sem.at[k],
            device_id=(gx, other),
            device_id_type=MESH,
        )

    def z_copy(d):
        to = (z + d) % NZ
        return pltpu.make_async_remote_copy(
            src_ref=zsend.at[to],
            dst_ref=zrecv.at[z],
            send_sem=zsend_sem,
            recv_sem=zrecv_sem,
            device_id=z_peer(to),
            device_id_type=MESH,
        )

    z_all = pltpu.make_async_remote_copy(
        src_ref=zsend.at[pl.ds(0, NZ - 1)],
        dst_ref=zrecv.at[pl.ds(0, NZ - 1)],
        send_sem=zsend_sem,
        recv_sem=zrecv_sem,
        device_id=(gx, other),
        device_id_type=MESH,
    )

    def compute(k):
        (w_lo, w_hi), (lo, hi) = CHUNKS[k]
        for n in range(w_lo, w_hi):
            w = ORDER[n]
            if RIM[w]:
                r = product(w, RIM[w])
                for jz in range(3):
                    taps[slot(n, jz)] += r[:, jz * C : (jz + 1) * C]

        @pl.loop(2 * lo, 2 * hi)
        def _(u):
            for h in range(2):
                a = jnp.concatenate(
                    [taps[2 * u, 64 * h : 64 * h + 64], taps[2 * u + 1, 64 * h : 64 * h + 64]], axis=0
                )
                t = a.T.reshape(NQ, 2, 8, C)
                parts[0, u, h] = t[:, 0]
                parts[1, u, h] = t[:, 1]

        sib_copy(k).start()

    def forward(k):
        lo, hi = CHUNKS[k][1]
        sib_copy(k).wait_recv()

        @pl.loop(lo, hi)
        def _(v):
            for h in range(2):
                both = [parts[core, 2 * v + e, h] + sib[2 * v + e, h] for e in range(2)]
                xsend[NQ * h : NQ * h + NQ, v] = jnp.concatenate(both, axis=1).astype(BF16)

        for d in XY:
            xy_copy(k, d).start()

    for step in STEPS:
        if step == "y":
            landed(False)

            @pl.loop(0, WX)
            def _(x):
                restack(1 + x, 0)
                restack(1 + x, WY + 1)
        elif step == "x":
            landed(True)

            @pl.loop(0, WY + 2)
            def _(y):
                restack(0, y)
                restack(WX + 1, y)
        elif step[0] == "c":
            compute(int(step[1]))
        else:
            forward(int(step[1]))

    load_ker.wait()
    acc[...] = jnp.zeros_like(acc)

    @pl.loop(0, 9)
    def _(w):
        wt = jnp.concatenate([wts[3 * w + jz] for jz in range(3)], axis=1)
        acc[...] += lax.dot_general(
            window(w), wt, (((1,), (1,)), ((), ())), preferred_element_type=F32
        )

    for x in range(WX):
        back = acc[pl.ds(x * WY * DZ, WY * DZ)]
        ig_ref[x] = (slope[x] * back).astype(BF16).reshape(WY, DZ, C)

    for k in range(len(CHUNKS)):
        xy_all(k).wait_recv()

    xrecv[here] = xsend[here]
    total = xrecv[0].astype(F32)
    for m in range(1, NXY):
        total = total + xrecv[m].astype(F32)
    sums[pl.ds(0, 8 * PAIRS)] = total.reshape(8 * PAIRS, C)
    sums[pl.ds(8 * PAIRS, C - 8 * PAIRS)] = jnp.zeros((C - 8 * PAIRS, C), F32)
    total = jnp.concatenate([sums[pl.ds(o, 16, stride=8)] for o in range(8)], axis=0)
    turned = total.T.reshape(2, NZ, 8, C)
    for e in range(2):
        zsend[:, e] = turned[e]

    for d in ZS:
        z_copy(d).start()
    zrecv[z] = zsend[z]

    for i, (dx, dy) in enumerate(DIRS):
        @pl.when(has(dx, gx, 16) * has(dy, gy, 16) == 1)
        def _():
            hop(i).wait_send()

    for k in range(len(CHUNKS)):
        sib_copy(k).wait_send()
        xy_all(k).wait_send()

    z_all.wait_recv()
    out = zrecv[0]
    for m in range(1, NZ):
        out = out + zrecv[m]
    kg_ref[...] = out
    z_all.wait_send()


def finish(ig_ref, sums_ref, out_ref, grad_ref, turn):
    out_ref[...] = ig_ref[...]
    total = sums_ref[...].reshape(16, C) / math.sqrt(32 * 64 * 48)
    for o in range(8):
        turn[pl.ds(o, 16, stride=8)] = pltpu.roll(total, (C - 16 * o) % C, 1)
    pair = turn[...].reshape(2, 8, 8, C)
    lane = lax.broadcasted_iota(jnp.int32, (8, C), 1)
    place = lane
    for n, w in enumerate(ORDER):
        place = jnp.where(lane // 3 == w, lane - 3 * w + slot(n, 0), place)
    source = jnp.minimum(place // 2, 15)
    for i in range(8):
        even = jnp.take_along_axis(pair[0, i], source, axis=1)
        odd = jnp.take_along_axis(pair[1, i], source, axis=1)
        grad_ref[i] = jnp.where(place % 2 == 0, even, odd)[:, :27]


def local(inputs, cotangent, kernel):
    n = len(CHUNKS)
    hbm = pl.BlockSpec(memory_space=pl.ANY)
    vmem = pl.BlockSpec(memory_space=pltpu.VMEM)
    dma = pltpu.SemaphoreType.DMA
    input_grad, sums = pl.pallas_call(
        body,
        out_shape=(
            jax.ShapeDtypeStruct((WX, WY, DZ, C), BF16),
            jax.ShapeDtypeStruct((2, 8, C), F32),
        ),
        in_specs=[hbm, hbm, hbm],
        out_specs=(vmem, vmem),
        scratch_shapes=[
            pltpu.VMEM((WX, WY, DZ, C), BF16),
            pltpu.VMEM((27, C, C), BF16),
            pltpu.VMEM((WX + 2, WY + 2, DZ, C), BF16),
            pltpu.VMEM((WX + 2, WY + 2, DZ, 3 * C), BF16),
            pltpu.VMEM((WX, WY, DZ, C), F32),
            pltpu.VMEM((WX, WY * DZ, C), F32),
            pltpu.VMEM((VOX, C), F32),
            pltpu.VMEM((28, C, C), F32),
            pltpu.VMEM((2, PAIRS, 2, NQ, 8, C), F32),
            pltpu.VMEM((PAIRS, 2, NQ, 8, C), F32),
            pltpu.VMEM((NXY, PAIRS // 2, 16, C), BF16),
            pltpu.VMEM((NXY, PAIRS // 2, 16, C), BF16),
            pltpu.VMEM((NZ, 2, 8, C), F32),
            pltpu.VMEM((NZ, 2, 8, C), F32),
            pltpu.VMEM((C, C), F32),
            dma((3,)),
            dma((8,)),
            dma((8,)),
            dma((n,)),
            dma((n,)),
            dma((n,)),
            dma((n,)),
            dma,
            dma,
        ],
        compiler_params=pltpu.CompilerParams(
            collective_id=0, has_side_effects=True, vmem_limit_bytes=32 * 1024 * 1024
        ),
        name="conv_backward",
    )(*(pltpu.with_memory_space_constraint(a, pltpu.HBM) for a in (inputs, cotangent, kernel)))
    whole = lambda shape: pl.BlockSpec(shape, lambda: (0,) * len(shape))
    input_grad, grad = pl.pallas_call(
        finish,
        out_shape=(
            jax.ShapeDtypeStruct((WX, WY, DZ, C), BF16),
            jax.ShapeDtypeStruct((8, 8, 27), F32),
        ),
        in_specs=[vmem, vmem],
        out_specs=(whole((WX, WY, DZ, C)), whole((8, 8, 27))),
        scratch_shapes=[pltpu.VMEM((C, C), F32)],
        compiler_params=pltpu.CompilerParams(vmem_limit_bytes=2 * 1024 * 1024),
        name="finish",
    )(input_grad, sums)
    return (input_grad, grad.transpose(2, 0, 1))


def solution(mesh):
    return jax.shard_map(
        local,
        mesh=mesh,
        in_specs=(P("gx", "gy", None, None), P("gx", "gy", None, None), P()),
        out_specs=(P("gx", "gy", None, None), P(None, "gx", "gy")),
        check_vma=False,
    )
```

```python
import math

import jax
import jax.numpy as jnp
from jax import lax
from jax.experimental import pallas as pl
from jax.experimental.pallas import tpu as pltpu
from jax.sharding import PartitionSpec as P

MESH = pl.DeviceIdType.MESH
F32 = jnp.float32
BF16 = jnp.bfloat16

WX, WY, DZ, C = 2, 4, 48, 128
VOX = WX * WY * DZ
NZ = 8
NQ = 8
NXY = 2 * NQ
PAIRS = 14
ORDER = (4, 3, 5, 0, 1, 2, 6, 7, 8)
CHUNKS = (((0, 1), (0, 1)), ((1, 3), (1, 2)), ((3, 6), (2, 4)), ((6, 9), (4, 7)))
STEPS = ('c0', 'f0', 'y', 'c1', 'x', 'c2', 'f1', 'c3', 'f2', 'f3')


def slot(n, jz):
    return 3 * n + jz + (1 if n else 0)


XY = sorted(
    ((dx, dy) for dx in range(4) for dy in range(4) if dx or dy),
    key=lambda d: -(min(d[0], 4 - d[0]) + min(d[1], 4 - d[1])),
)
ZS = (4, 3, 5, 2, 6, 1, 7)
ROW = ((2, 0), (1, 0), (3, 0))
COLUMN = ((0, 2), (0, 1), (0, 3))
NEAR_Z = (2, 6, 1, 7)
DIRS = tuple((dx, dy) for dx in (-1, 0, 1) for dy in (-1, 0, 1) if (dx, dy) != (0, 0))


def blocks(w, local):
    jx, jy = w // 3, w % 3
    every = [(x, y) for x in range(WX) for y in range(WY)]
    inside = [(x, y) for x, y in every if 1 <= x + 2 - jx <= WX and 1 <= y + 2 - jy <= WY]
    return inside if local else [b for b in every if b not in inside]


LOCAL = [blocks(w, True) for w in range(9)]
RIM = [blocks(w, False) for w in range(9)]


def rim(d, width, send):
    if d == 0:
        return (1, width) if not send else (0, width)
    if send:
        return (width - 1, 1) if d > 0 else (0, 1)
    return (0, 1) if d > 0 else (width + 1, 1)


def body(
    inp_hbm, cot_hbm, ker_hbm, ig_ref, kg_ref,
    inp, wts, halo, stack, act, slope, acc, taps, parts, sib, xsend, xrecv, zsend, zrecv, sums,
    load_sem, hsend_sem, hrecv_sem, ssend_sem, srecv_sem, xsend_sem, xrecv_sem, zsend_sem, zrecv_sem,
    plane_in, z_in,
):
    gx, gy = lax.axis_index("gx"), lax.axis_index("gy")
    core, q = gy % 2, gy // 2
    z, yh = gx % NZ, gx // NZ
    here = yh * NQ + q
    px, py = q % 4, yh * 2 + q // 4
    other = gy + 1 - 2 * core

    def xy_peer(d):
        x, y = (px + d[0]) % 4, (py + d[1]) % 4
        m = y * 4 + x
        return m, ((m // NQ) * NZ + z, (m % NQ) * 2 + core)

    def z_peer(k):
        return (yh * NZ + k, gy)

    barrier = pltpu.get_barrier_semaphore()

    def greet(dev):
        pl.semaphore_signal(barrier, inc=1, device_id=dev, device_id_type=MESH)

    for dx, dy in DIRS:
        greet(((gx + dx + 16) % 16, (gy + dy + 16) % 16))
    for d in (*ROW, *COLUMN):
        greet(xy_peer(d)[1])
    for d in NEAR_Z:
        greet(z_peer((z + d) % NZ))

    own = halo.at[pl.ds(1, WX), pl.ds(1, WY)]
    load_cot = pltpu.make_async_copy(cot_hbm, own, load_sem.at[0])
    load_inp = pltpu.make_async_copy(inp_hbm, inp, load_sem.at[1])
    load_ker = pltpu.make_async_copy(ker_hbm, wts, load_sem.at[2])
    load_cot.start()
    load_inp.start()
    load_ker.start()

    def has(d, at, size):
        if d == 0:
            return 1
        return jnp.where(at < size - 1, 1, 0) if d > 0 else jnp.where(at > 0, 1, 0)

    def hop(i):
        dx, dy = DIRS[i]
        sx, sy = rim(dx, WX, True), rim(dy, WY, True)
        lx, ly = rim(dx, WX, False), rim(dy, WY, False)
        return pltpu.make_async_remote_copy(
            src_ref=halo.at[pl.ds(1 + sx[0], sx[1]), pl.ds(1 + sy[0], sy[1])],
            dst_ref=halo.at[pl.ds(*lx), pl.ds(*ly)],
            send_sem=hsend_sem.at[i],
            recv_sem=hrecv_sem.at[i],
            device_id=((gx + dx + 16) % 16, (gy + dy + 16) % 16),
            device_id_type=MESH,
        )

    load_inp.wait()

    @pl.loop(0, WX)
    def _(x):
        v = inp[x].astype(F32).reshape(WY * DZ, C)
        cdf = 0.5 * (1.0 + lax.erf(v / math.sqrt(2.0)))
        slope[x] = cdf + v * jnp.exp(-0.5 * v * v) / math.sqrt(2.0 * math.pi)
        act[x] = (v * cdf).astype(BF16).astype(F32).reshape(WY, DZ, C)

    row = lax.broadcasted_iota(jnp.int32, (DZ, C), 0)

    def restack(x, y):
        v = halo[x, y].astype(F32)
        up = jnp.where(row == DZ - 1, 0.0, pltpu.roll(v, DZ - 1, 0))
        down = jnp.where(row == 0, 0.0, pltpu.roll(v, 1, 0))
        stack[x, y] = jnp.concatenate([up, v, down], axis=1).astype(BF16)

    load_cot.wait()

    @pl.loop(0, WX * WY)
    def _(k):
        restack(1 + k // WY, 1 + k % WY)

    def gather(lhs_blocks):
        return jnp.concatenate([act[x, y] for x, y in lhs_blocks], axis=0).T.astype(BF16)

    def product(w, chosen):
        jx, jy = w // 3, w % 3
        rows = [stack[x + 2 - jx, y + 2 - jy] for x, y in chosen]
        return jnp.dot(lhs[w, chosen is RIM[w]], jnp.concatenate(rows, axis=0), preferred_element_type=F32)

    lhs = {}
    for w in ORDER:
        lhs[w, False] = gather(LOCAL[w])
        if RIM[w]:
            lhs[w, True] = gather(RIM[w])
    for n, w in enumerate(ORDER):
        r = product(w, LOCAL[w])
        for jz in range(3):
            taps[slot(n, jz)] = r[:, jz * C : (jz + 1) * C]
    taps[3] = jnp.zeros((C, C), F32)
    pl.semaphore_wait(barrier, len(DIRS) + len(ROW) + len(COLUMN) + len(NEAR_Z))

    for i, (dx, dy) in enumerate(DIRS):
        @pl.when(has(dx, gx, 16) * has(dy, gy, 16) == 1)
        def _():
            hop(i).start()

    for d in ROW:
        pl.semaphore_signal(plane_in, inc=1, device_id=xy_peer(d)[1], device_id_type=MESH)
    for d in NEAR_Z:
        pl.semaphore_signal(z_in, inc=1, device_id=z_peer((z + d) % NZ), device_id_type=MESH)


    for i, (dx, dy) in enumerate(DIRS):
        lx, ly = rim(dx, WX, False), rim(dy, WY, False)

        @pl.when(has(-dx, gx, 16) * has(-dy, gy, 16) == 0)
        def _():
            halo[pl.ds(*lx), pl.ds(*ly)] = jnp.zeros((lx[1], ly[1], DZ, C), BF16)

    def landed(along_x):
        for i, (dx, dy) in enumerate(DIRS):
            if (dx != 0) != along_x:
                continue

            @pl.when(has(-dx, gx, 16) * has(-dy, gy, 16) == 1)
            def _():
                hop(i).wait_recv()

    def window(w):
        jx, jy = w // 3, w % 3
        return stack[pl.ds(2 - jx, WX), pl.ds(2 - jy, WY)].reshape(VOX, 3 * C)

    def sib_copy(k):
        lo, hi = CHUNKS[k][1]
        return pltpu.make_async_remote_copy(
            src_ref=parts.at[1 - core, pl.ds(2 * lo, 2 * (hi - lo))],
            dst_ref=sib.at[pl.ds(2 * lo, 2 * (hi - lo))],
            send_sem=ssend_sem.at[k],
            recv_sem=srecv_sem.at[k],
            device_id=(gx, other),
            device_id_type=MESH,
        )

    def xy_copy(k, d):
        lo, hi = CHUNKS[k][1]
        m, twin = xy_peer(d)
        return pltpu.make_async_remote_copy(
            src_ref=xsend.at[m, pl.ds(lo, hi - lo)],
            dst_ref=xrecv.at[here, pl.ds(lo, hi - lo)],
            send_sem=xsend_sem.at[k],
            recv_sem=xrecv_sem.at[k],
            device_id=twin,
            device_id_type=MESH,
        )

    def xy_all(k):
        lo, hi = CHUNKS[k][1]
        return pltpu.make_async_remote_copy(
            src_ref=xsend.at[pl.ds(0, NXY - 1), pl.ds(lo, hi - lo)],
            dst_ref=xrecv.at[pl.ds(0, NXY - 1), pl.ds(lo, hi - lo)],
            send_sem=xsend_sem.at[k],
            recv_sem=xrecv_sem.at[k],
            device_id=(gx, other),
            device_id_type=MESH,
        )

    def z_copy(d):
        to = (z + d) % NZ
        return pltpu.make_async_remote_copy(
            src_ref=zsend.at[to],
            dst_ref=zrecv.at[z],
            send_sem=zsend_sem,
            recv_sem=zrecv_sem,
            device_id=z_peer(to),
            device_id_type=MESH,
        )

    z_all = pltpu.make_async_remote_copy(
        src_ref=zsend.at[pl.ds(0, NZ - 1)],
        dst_ref=zrecv.at[pl.ds(0, NZ - 1)],
        send_sem=zsend_sem,
        recv_sem=zrecv_sem,
        device_id=(gx, other),
        device_id_type=MESH,
    )

    def compute(k):
        (w_lo, w_hi), (lo, hi) = CHUNKS[k]
        for n in range(w_lo, w_hi):
            w = ORDER[n]
            if RIM[w]:
                r = product(w, RIM[w])
                for jz in range(3):
                    taps[slot(n, jz)] += r[:, jz * C : (jz + 1) * C]

        for u in range(2 * lo, 2 * hi):
            for h in range(2):
                a = jnp.concatenate(
                    [taps[2 * u, 64 * h : 64 * h + 64], taps[2 * u + 1, 64 * h : 64 * h + 64]], axis=0
                )
                t = a.T.reshape(NQ, 2, 8, C)
                parts[0, u, h] = t[:, 0]
                parts[1, u, h] = t[:, 1]

        sib_copy(k).start()

    def forward(k):
        lo, hi = CHUNKS[k][1]
        sib_copy(k).wait_recv()

        @pl.loop(lo, hi)
        def _(v):
            for h in range(2):
                both = [parts[core, 2 * v + e, h] + sib[2 * v + e, h] for e in range(2)]
                xsend[NQ * h : NQ * h + NQ, v] = jnp.concatenate(both, axis=1).astype(BF16)

        if k == 0:
            pl.semaphore_wait(plane_in, len(ROW))
        for d in XY:
            xy_copy(k, d).start()

    for step in STEPS:
        if step == "y":
            landed(False)

            for x in range(WX):
                restack(1 + x, 0)
                restack(1 + x, WY + 1)
        elif step == "x":
            landed(True)

            for y in range(WY + 2):
                restack(0, y)
                restack(WX + 1, y)
        elif step[0] == "c":
            compute(int(step[1]))
        else:
            forward(int(step[1]))

    load_ker.wait()
    acc[...] = jnp.zeros_like(acc)

    @pl.loop(0, 9)
    def _(w):
        wt = jnp.concatenate([wts[3 * w + jz] for jz in range(3)], axis=1)
        acc[...] += lax.dot_general(
            window(w), wt, (((1,), (1,)), ((), ())), preferred_element_type=F32
        )

    for x in range(WX):
        back = acc[pl.ds(x * WY * DZ, WY * DZ)]
        ig_ref[x] = (slope[x] * back).astype(BF16).reshape(WY, DZ, C)

    for k in range(len(CHUNKS)):
        xy_all(k).wait_recv()

    xrecv[here] = xsend[here]
    total = xrecv[0].astype(F32)
    for m in range(1, NXY):
        total = total + xrecv[m].astype(F32)
    sums[pl.ds(0, 8 * PAIRS)] = total.reshape(8 * PAIRS, C)
    sums[pl.ds(8 * PAIRS, C - 8 * PAIRS)] = jnp.zeros((C - 8 * PAIRS, C), F32)
    total = jnp.concatenate([sums[pl.ds(o, 16, stride=8)] for o in range(8)], axis=0)
    turned = total.T.reshape(2, NZ, 8, C)
    for e in range(2):
        zsend[:, e] = turned[e]

    pl.semaphore_wait(z_in, len(NEAR_Z))
    for d in ZS:
        z_copy(d).start()
    zrecv[z] = zsend[z]

    for i, (dx, dy) in enumerate(DIRS):
        @pl.when(has(dx, gx, 16) * has(dy, gy, 16) == 1)
        def _():
            hop(i).wait_send()

    for k in range(len(CHUNKS)):
        sib_copy(k).wait_send()
        xy_all(k).wait_send()

    z_all.wait_recv()
    out = zrecv[0]
    for m in range(1, NZ):
        out = out + zrecv[m]
    kg_ref[...] = out
    z_all.wait_send()


def finish(ig_ref, sums_ref, out_ref, grad_ref, turn):
    out_ref[...] = ig_ref[...]
    total = sums_ref[...].reshape(16, C) / math.sqrt(32 * 64 * 48)
    for o in range(8):
        turn[pl.ds(o, 16, stride=8)] = pltpu.roll(total, (C - 16 * o) % C, 1)
    pair = turn[...].reshape(2, 8, 8, C)
    lane = lax.broadcasted_iota(jnp.int32, (8, C), 1)
    place = lane
    for n, w in enumerate(ORDER):
        place = jnp.where(lane // 3 == w, lane - 3 * w + slot(n, 0), place)
    source = jnp.minimum(place // 2, 15)
    for i in range(8):
        even = jnp.take_along_axis(pair[0, i], source, axis=1)
        odd = jnp.take_along_axis(pair[1, i], source, axis=1)
        grad_ref[i] = jnp.where(place % 2 == 0, even, odd)[:, :27]


def local(inputs, cotangent, kernel):
    n = len(CHUNKS)
    hbm = pl.BlockSpec(memory_space=pl.ANY)
    vmem = pl.BlockSpec(memory_space=pltpu.VMEM)
    dma = pltpu.SemaphoreType.DMA
    input_grad, sums = pl.pallas_call(
        body,
        out_shape=(
            jax.ShapeDtypeStruct((WX, WY, DZ, C), BF16),
            jax.ShapeDtypeStruct((2, 8, C), F32),
        ),
        in_specs=[hbm, hbm, hbm],
        out_specs=(vmem, vmem),
        scratch_shapes=[
            pltpu.VMEM((WX, WY, DZ, C), BF16),
            pltpu.VMEM((27, C, C), BF16),
            pltpu.VMEM((WX + 2, WY + 2, DZ, C), BF16),
            pltpu.VMEM((WX + 2, WY + 2, DZ, 3 * C), BF16),
            pltpu.VMEM((WX, WY, DZ, C), F32),
            pltpu.VMEM((WX, WY * DZ, C), F32),
            pltpu.VMEM((VOX, C), F32),
            pltpu.VMEM((28, C, C), F32),
            pltpu.VMEM((2, PAIRS, 2, NQ, 8, C), F32),
            pltpu.VMEM((PAIRS, 2, NQ, 8, C), F32),
            pltpu.VMEM((NXY, PAIRS // 2, 16, C), BF16),
            pltpu.VMEM((NXY, PAIRS // 2, 16, C), BF16),
            pltpu.VMEM((NZ, 2, 8, C), F32),
            pltpu.VMEM((NZ, 2, 8, C), F32),
            pltpu.VMEM((C, C), F32),
            dma((3,)),
            dma((8,)),
            dma((8,)),
            dma((n,)),
            dma((n,)),
            dma((n,)),
            dma((n,)),
            dma,
            dma,
            pltpu.SemaphoreType.REGULAR,
            pltpu.SemaphoreType.REGULAR,
        ],
        compiler_params=pltpu.CompilerParams(
            collective_id=0, has_side_effects=True, vmem_limit_bytes=32 * 1024 * 1024
        ),
        name="conv_backward",
    )(*(pltpu.with_memory_space_constraint(a, pltpu.HBM) for a in (inputs, cotangent, kernel)))
    whole = lambda shape: pl.BlockSpec(shape, lambda: (0,) * len(shape))
    input_grad, grad = pl.pallas_call(
        finish,
        out_shape=(
            jax.ShapeDtypeStruct((WX, WY, DZ, C), BF16),
            jax.ShapeDtypeStruct((8, 8, 27), F32),
        ),
        in_specs=[vmem, vmem],
        out_specs=(whole((WX, WY, DZ, C)), whole((8, 8, 27))),
        scratch_shapes=[pltpu.VMEM((C, C), F32)],
        compiler_params=pltpu.CompilerParams(vmem_limit_bytes=2 * 1024 * 1024),
        name="finish",
    )(input_grad, sums)
    return (input_grad, grad.transpose(2, 0, 1))


def solution(mesh):
    return jax.shard_map(
        local,
        mesh=mesh,
        in_specs=(P("gx", "gy", None, None), P("gx", "gy", None, None), P()),
        out_specs=(P("gx", "gy", None, None), P(None, "gx", "gy")),
        check_vma=False,
    )
```

```python
import math

import jax
import jax.numpy as jnp
from jax import lax
from jax.experimental import pallas as pl
from jax.experimental.pallas import tpu as pltpu
from jax.sharding import PartitionSpec as P

MESH = pl.DeviceIdType.MESH
F32 = jnp.float32
BF16 = jnp.bfloat16

WX, WY, DZ, C = 2, 4, 48, 128
VOX = WX * WY * DZ
NZ = 8
NQ = 8
NXY = 2 * NQ
PAIRS = 14
ORDER = (4, 3, 5, 6, 7, 8, 0, 1, 2)
CHUNKS = (((0, 1), (0, 1)), ((1, 3), (1, 2)), ((3, 5), (2, 4)), ((5, 9), (4, 7)))
STEPS = ("c0", "f0", "y", "c1", "m", "c2", "f1", "p", "c3", "f2", "f3")


def slot(n, jz):
    return 3 * n + jz + (1 if n else 0)


XY = sorted(
    ((dx, dy) for dx in range(4) for dy in range(4) if dx or dy),
    key=lambda d: -(min(d[0], 4 - d[0]) + min(d[1], 4 - d[1])),
)
ZS = (4, 3, 5, 2, 6, 1, 7)
ROW = ((2, 0), (1, 0), (3, 0))
COLUMN = ((0, 2), (0, 1), (0, 3))
NEAR_Z = (2, 6, 1, 7)
DIRS = tuple((dx, dy) for dx in (-1, 1, 0) for dy in (-1, 0, 1) if (dx, dy) != (0, 0))


def blocks(w, local):
    jx, jy = w // 3, w % 3
    every = [(x, y) for x in range(WX) for y in range(WY)]
    inside = [(x, y) for x, y in every if 1 <= x + 2 - jx <= WX and 1 <= y + 2 - jy <= WY]
    return inside if local else [b for b in every if b not in inside]


LOCAL = [blocks(w, True) for w in range(9)]
RIM = [blocks(w, False) for w in range(9)]


def rim(d, width, send):
    if d == 0:
        return (1, width) if not send else (0, width)
    if send:
        return (width - 1, 1) if d > 0 else (0, 1)
    return (0, 1) if d > 0 else (width + 1, 1)


def body(
    inp_hbm, cot_hbm, ker_hbm, ig_ref, kg_ref,
    inp, wts, halo, stack, act, slope, acc, taps, parts, sib, xsend, xrecv, zsend, zrecv, sums,
    load_sem, hsend_sem, hrecv_sem, ssend_sem, srecv_sem, xsend_sem, xrecv_sem, zsend_sem, zrecv_sem,
    plane_in, z_in,
):
    gx, gy = lax.axis_index("gx"), lax.axis_index("gy")
    core, q = gy % 2, gy // 2
    z, yh = gx % NZ, gx // NZ
    here = yh * NQ + q
    px, py = q % 4, yh * 2 + q // 4
    other = gy + 1 - 2 * core

    def xy_peer(d):
        x, y = (px + d[0]) % 4, (py + d[1]) % 4
        m = y * 4 + x
        return m, ((m // NQ) * NZ + z, (m % NQ) * 2 + core)

    def z_peer(k):
        return (yh * NZ + k, gy)

    barrier = pltpu.get_barrier_semaphore()

    def greet(dev):
        pl.semaphore_signal(barrier, inc=1, device_id=dev, device_id_type=MESH)

    for dx, dy in DIRS:
        greet(((gx + dx + 16) % 16, (gy + dy + 16) % 16))
    for d in (*ROW, *COLUMN):
        greet(xy_peer(d)[1])
    for d in NEAR_Z:
        greet(z_peer((z + d) % NZ))

    own = halo.at[pl.ds(1, WX), pl.ds(1, WY)]
    load_cot = pltpu.make_async_copy(cot_hbm, own, load_sem.at[0])
    load_inp = pltpu.make_async_copy(inp_hbm, inp, load_sem.at[1])
    load_ker = pltpu.make_async_copy(ker_hbm, wts, load_sem.at[2])
    load_cot.start()
    load_inp.start()
    load_ker.start()

    def has(d, at, size):
        if d == 0:
            return 1
        return jnp.where(at < size - 1, 1, 0) if d > 0 else jnp.where(at > 0, 1, 0)

    def hop(i):
        dx, dy = DIRS[i]
        sx, sy = rim(dx, WX, True), rim(dy, WY, True)
        lx, ly = rim(dx, WX, False), rim(dy, WY, False)
        return pltpu.make_async_remote_copy(
            src_ref=halo.at[pl.ds(1 + sx[0], sx[1]), pl.ds(1 + sy[0], sy[1])],
            dst_ref=halo.at[pl.ds(*lx), pl.ds(*ly)],
            send_sem=hsend_sem.at[i],
            recv_sem=hrecv_sem.at[i],
            device_id=((gx + dx + 16) % 16, (gy + dy + 16) % 16),
            device_id_type=MESH,
        )

    load_inp.wait()

    @pl.loop(0, WX)
    def _(x):
        v = inp[x].astype(F32).reshape(WY * DZ, C)
        cdf = 0.5 * (1.0 + lax.erf(v / math.sqrt(2.0)))
        slope[x] = cdf + v * jnp.exp(-0.5 * v * v) / math.sqrt(2.0 * math.pi)
        act[x] = (v * cdf).astype(BF16).astype(F32).reshape(WY, DZ, C)

    row = lax.broadcasted_iota(jnp.int32, (DZ, C), 0)

    def restack(x, y):
        v = halo[x, y].astype(F32)
        up = jnp.where(row == DZ - 1, 0.0, pltpu.roll(v, DZ - 1, 0))
        down = jnp.where(row == 0, 0.0, pltpu.roll(v, 1, 0))
        stack[x, y] = jnp.concatenate([up, v, down], axis=1).astype(BF16)

    load_cot.wait()

    @pl.loop(0, WX * WY)
    def _(k):
        restack(1 + k // WY, 1 + k % WY)

    def gather(lhs_blocks):
        return jnp.concatenate([act[x, y] for x, y in lhs_blocks], axis=0).T.astype(BF16)

    def product(w, chosen):
        jx, jy = w // 3, w % 3
        rows = [stack[x + 2 - jx, y + 2 - jy] for x, y in chosen]
        return jnp.dot(lhs[w, chosen is RIM[w]], jnp.concatenate(rows, axis=0), preferred_element_type=F32)

    lhs = {}
    for w in ORDER:
        lhs[w, False] = gather(LOCAL[w])
        if RIM[w]:
            lhs[w, True] = gather(RIM[w])
    for n, w in enumerate(ORDER):
        r = product(w, LOCAL[w])
        for jz in range(3):
            taps[slot(n, jz)] = r[:, jz * C : (jz + 1) * C]
    taps[3] = jnp.zeros((C, C), F32)
    pl.semaphore_wait(barrier, len(DIRS) + len(ROW) + len(COLUMN) + len(NEAR_Z))

    for i, (dx, dy) in enumerate(DIRS):
        @pl.when(has(dx, gx, 16) * has(dy, gy, 16) == 1)
        def _():
            hop(i).start()

    for d in ROW:
        pl.semaphore_signal(plane_in, inc=1, device_id=xy_peer(d)[1], device_id_type=MESH)
    for d in NEAR_Z:
        pl.semaphore_signal(z_in, inc=1, device_id=z_peer((z + d) % NZ), device_id_type=MESH)


    for i, (dx, dy) in enumerate(DIRS):
        lx, ly = rim(dx, WX, False), rim(dy, WY, False)

        @pl.when(has(-dx, gx, 16) * has(-dy, gy, 16) == 0)
        def _():
            halo[pl.ds(*lx), pl.ds(*ly)] = jnp.zeros((lx[1], ly[1], DZ, C), BF16)

    def landed(along):
        for i, (dx, dy) in enumerate(DIRS):
            if dx != along:
                continue

            @pl.when(has(-dx, gx, 16) * has(-dy, gy, 16) == 1)
            def _():
                hop(i).wait_recv()

    def window(w):
        jx, jy = w // 3, w % 3
        return stack[pl.ds(2 - jx, WX), pl.ds(2 - jy, WY)].reshape(VOX, 3 * C)

    def sib_copy(v):
        return pltpu.make_async_remote_copy(
            src_ref=parts.at[1 - core, pl.ds(2 * v, 2)],
            dst_ref=sib.at[pl.ds(2 * v, 2)],
            send_sem=ssend_sem.at[v],
            recv_sem=srecv_sem.at[v],
            device_id=(gx, other),
            device_id_type=MESH,
        )

    def xy_copy(k, d):
        lo, hi = CHUNKS[k][1]
        m, twin = xy_peer(d)
        return pltpu.make_async_remote_copy(
            src_ref=xsend.at[m, pl.ds(lo, hi - lo)],
            dst_ref=xrecv.at[here, pl.ds(lo, hi - lo)],
            send_sem=xsend_sem.at[k],
            recv_sem=xrecv_sem.at[k],
            device_id=twin,
            device_id_type=MESH,
        )

    def xy_all(k):
        lo, hi = CHUNKS[k][1]
        return pltpu.make_async_remote_copy(
            src_ref=xsend.at[pl.ds(0, NXY - 1), pl.ds(lo, hi - lo)],
            dst_ref=xrecv.at[pl.ds(0, NXY - 1), pl.ds(lo, hi - lo)],
            send_sem=xsend_sem.at[k],
            recv_sem=xrecv_sem.at[k],
            device_id=(gx, other),
            device_id_type=MESH,
        )

    def z_copy(d):
        to = (z + d) % NZ
        return pltpu.make_async_remote_copy(
            src_ref=zsend.at[to],
            dst_ref=zrecv.at[z],
            send_sem=zsend_sem,
            recv_sem=zrecv_sem,
            device_id=z_peer(to),
            device_id_type=MESH,
        )

    z_all = pltpu.make_async_remote_copy(
        src_ref=zsend.at[pl.ds(0, NZ - 1)],
        dst_ref=zrecv.at[pl.ds(0, NZ - 1)],
        send_sem=zsend_sem,
        recv_sem=zrecv_sem,
        device_id=(gx, other),
        device_id_type=MESH,
    )

    def turn(v):
        for u in (2 * v, 2 * v + 1):
            for h in range(2):
                a = jnp.concatenate(
                    [taps[2 * u, 64 * h : 64 * h + 64], taps[2 * u + 1, 64 * h : 64 * h + 64]], axis=0
                )
                t = a.T.reshape(NQ, 2, 8, C)
                parts[0, u, h] = t[:, 0]
                parts[1, u, h] = t[:, 1]
        sib_copy(v).start()

    def compute(k):
        (w_lo, w_hi), (lo, hi) = CHUNKS[k]
        done = lo
        for n in range(w_lo, w_hi):
            w = ORDER[n]
            if RIM[w]:
                r = product(w, RIM[w])
                for jz in range(3):
                    taps[slot(n, jz)] += r[:, jz * C : (jz + 1) * C]
            ready = min(hi, (slot(n, 2) + (2 if n == 0 else 1)) // 4)
            for v in range(done, ready):
                turn(v)
            done = max(done, ready)

    def forward(k):
        lo, hi = CHUNKS[k][1]
        for v in range(lo, hi):
            sib_copy(v).wait_recv()
            for h in range(2):
                both = [parts[core, 2 * v + e, h] + sib[2 * v + e, h] for e in range(2)]
                xsend[NQ * h : NQ * h + NQ, v] = jnp.concatenate(both, axis=1).astype(BF16)
        if k == 0:
            pl.semaphore_wait(plane_in, len(ROW))
        for d in XY:
            xy_copy(k, d).start()
        xrecv[here, lo:hi] = xsend[here, lo:hi]

    for step in STEPS:
        if step == "y":
            landed(0)
            for x in range(WX):
                restack(1 + x, 0)
                restack(1 + x, WY + 1)
        elif step == "m":
            landed(1)
            for y in range(WY + 2):
                restack(0, y)
        elif step == "p":
            landed(-1)
            for y in range(WY + 2):
                restack(WX + 1, y)
        elif step[0] == "c":
            compute(int(step[1]))
        else:
            forward(int(step[1]))

    load_ker.wait()
    acc[...] = jnp.zeros_like(acc)

    @pl.loop(0, 9)
    def _(w):
        wt = jnp.concatenate([wts[3 * w + jz] for jz in range(3)], axis=1)
        acc[...] += lax.dot_general(
            window(w), wt, (((1,), (1,)), ((), ())), preferred_element_type=F32
        )

    for x in range(WX):
        back = acc[pl.ds(x * WY * DZ, WY * DZ)]
        ig_ref[x] = (slope[x] * back).astype(BF16).reshape(WY, DZ, C)

    for k in range(len(CHUNKS)):
        lo, hi = CHUNKS[k][1]
        xy_all(k).wait_recv()
        total = xrecv[0, lo:hi].astype(F32)
        for m in range(1, NXY):
            total = total + xrecv[m, lo:hi].astype(F32)
        sums[pl.ds(16 * lo, 16 * (hi - lo))] = total.reshape(16 * (hi - lo), C)
    sums[pl.ds(8 * PAIRS, C - 8 * PAIRS)] = jnp.zeros((C - 8 * PAIRS, C), F32)
    total = jnp.concatenate([sums[pl.ds(o, 16, stride=8)] for o in range(8)], axis=0)
    turned = total.T.reshape(2, NZ, 8, C)
    for e in range(2):
        zsend[:, e] = turned[e]

    pl.semaphore_wait(z_in, len(NEAR_Z))
    for d in ZS:
        z_copy(d).start()
    zrecv[z] = zsend[z]

    for i, (dx, dy) in enumerate(DIRS):
        @pl.when(has(dx, gx, 16) * has(dy, gy, 16) == 1)
        def _():
            hop(i).wait_send()

    for k in range(len(CHUNKS)):
        xy_all(k).wait_send()
    for v in range(PAIRS // 2):
        sib_copy(v).wait_send()

    z_all.wait_recv()
    out = zrecv[0]
    for m in range(1, NZ):
        out = out + zrecv[m]
    kg_ref[...] = out
    z_all.wait_send()


def finish(ig_ref, sums_ref, out_ref, grad_ref, turn):
    out_ref[...] = ig_ref[...]
    total = sums_ref[...].reshape(16, C) / math.sqrt(32 * 64 * 48)
    for o in range(8):
        turn[pl.ds(o, 16, stride=8)] = pltpu.roll(total, (C - 16 * o) % C, 1)
    pair = turn[...].reshape(2, 8, 8, C)
    lane = lax.broadcasted_iota(jnp.int32, (8, C), 1)
    place = lane
    for n, w in enumerate(ORDER):
        place = jnp.where(lane // 3 == w, lane - 3 * w + slot(n, 0), place)
    source = jnp.minimum(place // 2, 15)
    for i in range(8):
        even = jnp.take_along_axis(pair[0, i], source, axis=1)
        odd = jnp.take_along_axis(pair[1, i], source, axis=1)
        grad_ref[i] = jnp.where(place % 2 == 0, even, odd)[:, :27]


def local(inputs, cotangent, kernel):
    n = len(CHUNKS)
    hbm = pl.BlockSpec(memory_space=pl.ANY)
    vmem = pl.BlockSpec(memory_space=pltpu.VMEM)
    dma = pltpu.SemaphoreType.DMA
    input_grad, sums = pl.pallas_call(
        body,
        out_shape=(
            jax.ShapeDtypeStruct((WX, WY, DZ, C), BF16),
            jax.ShapeDtypeStruct((2, 8, C), F32),
        ),
        in_specs=[hbm, hbm, hbm],
        out_specs=(vmem, vmem),
        scratch_shapes=[
            pltpu.VMEM((WX, WY, DZ, C), BF16),
            pltpu.VMEM((27, C, C), BF16),
            pltpu.VMEM((WX + 2, WY + 2, DZ, C), BF16),
            pltpu.VMEM((WX + 2, WY + 2, DZ, 3 * C), BF16),
            pltpu.VMEM((WX, WY, DZ, C), F32),
            pltpu.VMEM((WX, WY * DZ, C), F32),
            pltpu.VMEM((VOX, C), F32),
            pltpu.VMEM((28, C, C), F32),
            pltpu.VMEM((2, PAIRS, 2, NQ, 8, C), F32),
            pltpu.VMEM((PAIRS, 2, NQ, 8, C), F32),
            pltpu.VMEM((NXY, PAIRS // 2, 16, C), BF16),
            pltpu.VMEM((NXY, PAIRS // 2, 16, C), BF16),
            pltpu.VMEM((NZ, 2, 8, C), F32),
            pltpu.VMEM((NZ, 2, 8, C), F32),
            pltpu.VMEM((C, C), F32),
            dma((3,)),
            dma((8,)),
            dma((8,)),
            dma((PAIRS // 2,)),
            dma((PAIRS // 2,)),
            dma((n,)),
            dma((n,)),
            dma,
            dma,
            pltpu.SemaphoreType.REGULAR,
            pltpu.SemaphoreType.REGULAR,
        ],
        compiler_params=pltpu.CompilerParams(
            collective_id=0, has_side_effects=True, vmem_limit_bytes=32 * 1024 * 1024
        ),
        name="conv_backward",
    )(*(pltpu.with_memory_space_constraint(a, pltpu.HBM) for a in (inputs, cotangent, kernel)))
    whole = lambda shape: pl.BlockSpec(shape, lambda: (0,) * len(shape))
    input_grad, grad = pl.pallas_call(
        finish,
        out_shape=(
            jax.ShapeDtypeStruct((WX, WY, DZ, C), BF16),
            jax.ShapeDtypeStruct((8, 8, 27), F32),
        ),
        in_specs=[vmem, vmem],
        out_specs=(whole((WX, WY, DZ, C)), whole((8, 8, 27))),
        scratch_shapes=[pltpu.VMEM((C, C), F32)],
        compiler_params=pltpu.CompilerParams(vmem_limit_bytes=2 * 1024 * 1024),
        name="finish",
    )(input_grad, sums)
    return (input_grad, grad.transpose(2, 0, 1))


def solution(mesh):
    return jax.shard_map(
        local,
        mesh=mesh,
        in_specs=(P("gx", "gy", None, None), P("gx", "gy", None, None), P()),
        out_specs=(P("gx", "gy", None, None), P(None, "gx", "gy")),
        check_vma=False,
    )
```

```python
import math

import jax
import jax.numpy as jnp
from jax import lax
from jax.experimental import pallas as pl
from jax.experimental.pallas import tpu as pltpu
from jax.sharding import PartitionSpec as P

MESH = pl.DeviceIdType.MESH
F32 = jnp.float32
BF16 = jnp.bfloat16

WX, WY, DZ, C = 2, 4, 48, 128
VOX = WX * WY * DZ
NZ = 8
NQ = 8
NXY = 2 * NQ
PAIRS = 14
ORDER = (4, 3, 5, 6, 7, 8, 0, 1, 2)
PRODUCTS = (((0, 1), (0, 1)), ((1, 3), (1, 2)), ((3, 5), (2, 4)), ((5, 7), (4, 5)), ((7, 9), (5, 7)))
CHUNKS = ((0, 2), (2, 4), (4, 7))
STEPS = ('c0', 'y', 'c1', 'm', 'c2', 'f0', 'p', 'c3', 'f1', 'c4', 'f2')


def slot(n, jz):
    return 3 * n + jz + (1 if n else 0)


XY = sorted(
    ((dx, dy) for dx in range(4) for dy in range(4) if dx or dy),
    key=lambda d: -(min(d[0], 4 - d[0]) + min(d[1], 4 - d[1])),
)
ZS = (4, 3, 5, 2, 6, 1, 7)
ROW = ((2, 0), (1, 0), (3, 0))
COLUMN = ((0, 2), (0, 1), (0, 3))
NEAR_Z = (2, 6, 1, 7)
DIRS = tuple((dx, dy) for dx in (-1, 1, 0) for dy in (-1, 0, 1) if (dx, dy) != (0, 0))


def blocks(w, local):
    jx, jy = w // 3, w % 3
    every = [(x, y) for x in range(WX) for y in range(WY)]
    inside = [(x, y) for x, y in every if 1 <= x + 2 - jx <= WX and 1 <= y + 2 - jy <= WY]
    return inside if local else [b for b in every if b not in inside]


LOCAL = [blocks(w, True) for w in range(9)]
RIM = [blocks(w, False) for w in range(9)]


def rim(d, width, send):
    if d == 0:
        return (1, width) if not send else (0, width)
    if send:
        return (width - 1, 1) if d > 0 else (0, 1)
    return (0, 1) if d > 0 else (width + 1, 1)


def body(
    inp_hbm, cot_hbm, ker_hbm, ig_ref, kg_ref,
    inp, wts, halo, stack, act, slope, acc, taps, parts, sib, xsend, xrecv, zsend, zrecv, sums,
    load_sem, hsend_sem, hrecv_sem, ssend_sem, srecv_sem, xsend_sem, xrecv_sem, zsend_sem, zrecv_sem,
    plane_in, z_in,
):
    gx, gy = lax.axis_index("gx"), lax.axis_index("gy")
    core, q = gy % 2, gy // 2
    z, yh = gx % NZ, gx // NZ
    here = yh * NQ + q
    px, py = q % 4, yh * 2 + q // 4
    other = gy + 1 - 2 * core

    def xy_peer(d):
        x, y = (px + d[0]) % 4, (py + d[1]) % 4
        m = y * 4 + x
        return m, ((m // NQ) * NZ + z, (m % NQ) * 2 + core)

    def z_peer(k):
        return (yh * NZ + k, gy)

    barrier = pltpu.get_barrier_semaphore()

    def greet(dev):
        pl.semaphore_signal(barrier, inc=1, device_id=dev, device_id_type=MESH)

    for dx, dy in DIRS:
        greet(((gx + dx + 16) % 16, (gy + dy + 16) % 16))
    for d in (*ROW, *COLUMN):
        greet(xy_peer(d)[1])
    for d in NEAR_Z:
        greet(z_peer((z + d) % NZ))

    own = halo.at[pl.ds(1, WX), pl.ds(1, WY)]
    load_cot = pltpu.make_async_copy(cot_hbm, own, load_sem.at[0])
    load_inp = pltpu.make_async_copy(inp_hbm, inp, load_sem.at[1])
    load_ker = pltpu.make_async_copy(ker_hbm, wts, load_sem.at[2])
    load_cot.start()
    load_inp.start()
    load_ker.start()

    def has(d, at, size):
        if d == 0:
            return 1
        return jnp.where(at < size - 1, 1, 0) if d > 0 else jnp.where(at > 0, 1, 0)

    def hop(i):
        dx, dy = DIRS[i]
        sx, sy = rim(dx, WX, True), rim(dy, WY, True)
        lx, ly = rim(dx, WX, False), rim(dy, WY, False)
        return pltpu.make_async_remote_copy(
            src_ref=halo.at[pl.ds(1 + sx[0], sx[1]), pl.ds(1 + sy[0], sy[1])],
            dst_ref=halo.at[pl.ds(*lx), pl.ds(*ly)],
            send_sem=hsend_sem.at[i],
            recv_sem=hrecv_sem.at[i],
            device_id=((gx + dx + 16) % 16, (gy + dy + 16) % 16),
            device_id_type=MESH,
        )

    load_inp.wait()

    @pl.loop(0, WX)
    def _(x):
        v = inp[x].astype(F32).reshape(WY * DZ, C)
        cdf = 0.5 * (1.0 + lax.erf(v / math.sqrt(2.0)))
        slope[x] = cdf + v * jnp.exp(-0.5 * v * v) / math.sqrt(2.0 * math.pi)
        act[x] = (v * cdf).astype(BF16).astype(F32).reshape(WY, DZ, C)

    row = lax.broadcasted_iota(jnp.int32, (DZ, C), 0)

    def restack(x, y):
        v = halo[x, y].astype(F32)
        up = jnp.where(row == DZ - 1, 0.0, pltpu.roll(v, DZ - 1, 0))
        down = jnp.where(row == 0, 0.0, pltpu.roll(v, 1, 0))
        stack[x, y] = jnp.concatenate([up, v, down], axis=1).astype(BF16)

    load_cot.wait()

    @pl.loop(0, WX * WY)
    def _(k):
        restack(1 + k // WY, 1 + k % WY)

    def gather(lhs_blocks):
        return jnp.concatenate([act[x, y] for x, y in lhs_blocks], axis=0).T.astype(BF16)

    def product(w, chosen):
        jx, jy = w // 3, w % 3
        rows = [stack[x + 2 - jx, y + 2 - jy] for x, y in chosen]
        return jnp.dot(lhs[w, chosen is RIM[w]], jnp.concatenate(rows, axis=0), preferred_element_type=F32)

    lhs = {}
    for w in ORDER:
        lhs[w, False] = gather(LOCAL[w])
        if RIM[w]:
            lhs[w, True] = gather(RIM[w])
    for n, w in enumerate(ORDER):
        r = product(w, LOCAL[w])
        for jz in range(3):
            taps[slot(n, jz)] = r[:, jz * C : (jz + 1) * C]
    taps[3] = jnp.zeros((C, C), F32)
    pl.semaphore_wait(barrier, len(DIRS) + len(ROW) + len(COLUMN) + len(NEAR_Z))

    for i, (dx, dy) in enumerate(DIRS):
        @pl.when(has(dx, gx, 16) * has(dy, gy, 16) == 1)
        def _():
            hop(i).start()

    for d in ROW:
        pl.semaphore_signal(plane_in, inc=1, device_id=xy_peer(d)[1], device_id_type=MESH)
    for d in NEAR_Z:
        pl.semaphore_signal(z_in, inc=1, device_id=z_peer((z + d) % NZ), device_id_type=MESH)


    for i, (dx, dy) in enumerate(DIRS):
        lx, ly = rim(dx, WX, False), rim(dy, WY, False)

        @pl.when(has(-dx, gx, 16) * has(-dy, gy, 16) == 0)
        def _():
            halo[pl.ds(*lx), pl.ds(*ly)] = jnp.zeros((lx[1], ly[1], DZ, C), BF16)

    def landed(along):
        for i, (dx, dy) in enumerate(DIRS):
            if dx != along:
                continue

            @pl.when(has(-dx, gx, 16) * has(-dy, gy, 16) == 1)
            def _():
                hop(i).wait_recv()

    def window(w):
        jx, jy = w // 3, w % 3
        return stack[pl.ds(2 - jx, WX), pl.ds(2 - jy, WY)].reshape(VOX, 3 * C)

    def sib_copy(v):
        return pltpu.make_async_remote_copy(
            src_ref=parts.at[1 - core, pl.ds(2 * v, 2)],
            dst_ref=sib.at[pl.ds(2 * v, 2)],
            send_sem=ssend_sem.at[v],
            recv_sem=srecv_sem.at[v],
            device_id=(gx, other),
            device_id_type=MESH,
        )

    def xy_copy(k, d):
        lo, hi = CHUNKS[k]
        m, twin = xy_peer(d)
        return pltpu.make_async_remote_copy(
            src_ref=xsend.at[m, pl.ds(lo, hi - lo)],
            dst_ref=xrecv.at[here, pl.ds(lo, hi - lo)],
            send_sem=xsend_sem.at[k],
            recv_sem=xrecv_sem.at[k],
            device_id=twin,
            device_id_type=MESH,
        )

    def xy_all(k):
        lo, hi = CHUNKS[k]
        return pltpu.make_async_remote_copy(
            src_ref=xsend.at[pl.ds(0, NXY - 1), pl.ds(lo, hi - lo)],
            dst_ref=xrecv.at[pl.ds(0, NXY - 1), pl.ds(lo, hi - lo)],
            send_sem=xsend_sem.at[k],
            recv_sem=xrecv_sem.at[k],
            device_id=(gx, other),
            device_id_type=MESH,
        )

    def z_copy(d):
        to = (z + d) % NZ
        return pltpu.make_async_remote_copy(
            src_ref=zsend.at[to],
            dst_ref=zrecv.at[z],
            send_sem=zsend_sem,
            recv_sem=zrecv_sem,
            device_id=z_peer(to),
            device_id_type=MESH,
        )

    z_all = pltpu.make_async_remote_copy(
        src_ref=zsend.at[pl.ds(0, NZ - 1)],
        dst_ref=zrecv.at[pl.ds(0, NZ - 1)],
        send_sem=zsend_sem,
        recv_sem=zrecv_sem,
        device_id=(gx, other),
        device_id_type=MESH,
    )

    def turn(v):
        for u in (2 * v, 2 * v + 1):
            for h in range(2):
                a = jnp.concatenate(
                    [taps[2 * u, 64 * h : 64 * h + 64], taps[2 * u + 1, 64 * h : 64 * h + 64]], axis=0
                )
                t = a.T.reshape(NQ, 2, 8, C)
                parts[0, u, h] = t[:, 0]
                parts[1, u, h] = t[:, 1]
        sib_copy(v).start()

    def compute(k):
        (w_lo, w_hi), (lo, hi) = PRODUCTS[k]
        done = lo
        for n in range(w_lo, w_hi):
            w = ORDER[n]
            if RIM[w]:
                r = product(w, RIM[w])
                for jz in range(3):
                    taps[slot(n, jz)] += r[:, jz * C : (jz + 1) * C]
            ready = min(hi, (slot(n, 2) + (2 if n == 0 else 1)) // 4)
            for v in range(done, ready):
                turn(v)
            done = max(done, ready)

    def forward(k):
        lo, hi = CHUNKS[k]
        for v in range(lo, hi):
            sib_copy(v).wait_recv()
            for h in range(2):
                both = [parts[core, 2 * v + e, h] + sib[2 * v + e, h] for e in range(2)]
                xsend[NQ * h : NQ * h + NQ, v] = jnp.concatenate(both, axis=1).astype(BF16)
        if k == 0:
            pl.semaphore_wait(plane_in, len(ROW))
        for d in XY:
            xy_copy(k, d).start()
        xrecv[here, lo:hi] = xsend[here, lo:hi]

    for step in STEPS:
        if step == "y":
            landed(0)
            for x in range(WX):
                restack(1 + x, 0)
                restack(1 + x, WY + 1)
        elif step == "m":
            landed(1)
            for y in range(WY + 2):
                restack(0, y)
        elif step == "p":
            landed(-1)
            for y in range(WY + 2):
                restack(WX + 1, y)
        elif step[0] == "c":
            compute(int(step[1]))
        else:
            forward(int(step[1]))

    load_ker.wait()
    acc[...] = jnp.zeros_like(acc)

    @pl.loop(0, 9)
    def _(w):
        wt = jnp.concatenate([wts[3 * w + jz] for jz in range(3)], axis=1)
        acc[...] += lax.dot_general(
            window(w), wt, (((1,), (1,)), ((), ())), preferred_element_type=F32
        )

    for x in range(WX):
        back = acc[pl.ds(x * WY * DZ, WY * DZ)]
        ig_ref[x] = (slope[x] * back).astype(BF16).reshape(WY, DZ, C)

    for k in range(len(CHUNKS)):
        lo, hi = CHUNKS[k]
        xy_all(k).wait_recv()
        total = xrecv[0, lo:hi].astype(F32)
        for m in range(1, NXY):
            total = total + xrecv[m, lo:hi].astype(F32)
        sums[pl.ds(16 * lo, 16 * (hi - lo))] = total.reshape(16 * (hi - lo), C)
    sums[pl.ds(8 * PAIRS, C - 8 * PAIRS)] = jnp.zeros((C - 8 * PAIRS, C), F32)
    total = jnp.concatenate([sums[pl.ds(o, 16, stride=8)] for o in range(8)], axis=0)
    turned = total.T.reshape(2, NZ, 8, C)
    for e in range(2):
        zsend[:, e] = turned[e]

    pl.semaphore_wait(z_in, len(NEAR_Z))
    for d in ZS:
        z_copy(d).start()
    zrecv[z] = zsend[z]

    for i, (dx, dy) in enumerate(DIRS):
        @pl.when(has(dx, gx, 16) * has(dy, gy, 16) == 1)
        def _():
            hop(i).wait_send()

    for k in range(len(CHUNKS)):
        xy_all(k).wait_send()
    for v in range(PAIRS // 2):
        sib_copy(v).wait_send()

    z_all.wait_recv()
    out = zrecv[0]
    for m in range(1, NZ):
        out = out + zrecv[m]
    kg_ref[...] = out
    z_all.wait_send()


def finish(ig_ref, sums_ref, out_ref, grad_ref, turn):
    out_ref[...] = ig_ref[...]
    total = sums_ref[...].reshape(16, C) / math.sqrt(32 * 64 * 48)
    for o in range(8):
        turn[pl.ds(o, 16, stride=8)] = pltpu.roll(total, (C - 16 * o) % C, 1)
    pair = turn[...].reshape(2, 8, 8, C)
    lane = lax.broadcasted_iota(jnp.int32, (8, C), 1)
    place = lane
    for n, w in enumerate(ORDER):
        place = jnp.where(lane // 3 == w, lane - 3 * w + slot(n, 0), place)
    source = jnp.minimum(place // 2, 15)
    for i in range(8):
        even = jnp.take_along_axis(pair[0, i], source, axis=1)
        odd = jnp.take_along_axis(pair[1, i], source, axis=1)
        grad_ref[i] = jnp.where(place % 2 == 0, even, odd)[:, :27]


def local(inputs, cotangent, kernel):
    n = len(CHUNKS)
    hbm = pl.BlockSpec(memory_space=pl.ANY)
    vmem = pl.BlockSpec(memory_space=pltpu.VMEM)
    dma = pltpu.SemaphoreType.DMA
    input_grad, sums = pl.pallas_call(
        body,
        out_shape=(
            jax.ShapeDtypeStruct((WX, WY, DZ, C), BF16),
            jax.ShapeDtypeStruct((2, 8, C), F32),
        ),
        in_specs=[hbm, hbm, hbm],
        out_specs=(vmem, vmem),
        scratch_shapes=[
            pltpu.VMEM((WX, WY, DZ, C), BF16),
            pltpu.VMEM((27, C, C), BF16),
            pltpu.VMEM((WX + 2, WY + 2, DZ, C), BF16),
            pltpu.VMEM((WX + 2, WY + 2, DZ, 3 * C), BF16),
            pltpu.VMEM((WX, WY, DZ, C), F32),
            pltpu.VMEM((WX, WY * DZ, C), F32),
            pltpu.VMEM((VOX, C), F32),
            pltpu.VMEM((28, C, C), F32),
            pltpu.VMEM((2, PAIRS, 2, NQ, 8, C), F32),
            pltpu.VMEM((PAIRS, 2, NQ, 8, C), F32),
            pltpu.VMEM((NXY, PAIRS // 2, 16, C), BF16),
            pltpu.VMEM((NXY, PAIRS // 2, 16, C), BF16),
            pltpu.VMEM((NZ, 2, 8, C), F32),
            pltpu.VMEM((NZ, 2, 8, C), F32),
            pltpu.VMEM((C, C), F32),
            dma((3,)),
            dma((8,)),
            dma((8,)),
            dma((PAIRS // 2,)),
            dma((PAIRS // 2,)),
            dma((n,)),
            dma((n,)),
            dma,
            dma,
            pltpu.SemaphoreType.REGULAR,
            pltpu.SemaphoreType.REGULAR,
        ],
        compiler_params=pltpu.CompilerParams(
            collective_id=0, has_side_effects=True, vmem_limit_bytes=32 * 1024 * 1024
        ),
        name="conv_backward",
    )(*(pltpu.with_memory_space_constraint(a, pltpu.HBM) for a in (inputs, cotangent, kernel)))
    whole = lambda shape: pl.BlockSpec(shape, lambda: (0,) * len(shape))
    input_grad, grad = pl.pallas_call(
        finish,
        out_shape=(
            jax.ShapeDtypeStruct((WX, WY, DZ, C), BF16),
            jax.ShapeDtypeStruct((8, 8, 27), F32),
        ),
        in_specs=[vmem, vmem],
        out_specs=(whole((WX, WY, DZ, C)), whole((8, 8, 27))),
        scratch_shapes=[pltpu.VMEM((C, C), F32)],
        compiler_params=pltpu.CompilerParams(vmem_limit_bytes=2 * 1024 * 1024),
        name="finish",
    )(input_grad, sums)
    return (input_grad, grad.transpose(2, 0, 1))


def solution(mesh):
    return jax.shard_map(
        local,
        mesh=mesh,
        in_specs=(P("gx", "gy", None, None), P("gx", "gy", None, None), P()),
        out_specs=(P("gx", "gy", None, None), P(None, "gx", "gy")),
        check_vma=False,
    )
```

```python
import math

import jax
import jax.numpy as jnp
from jax import lax
from jax.experimental import pallas as pl
from jax.experimental.pallas import tpu as pltpu
from jax.sharding import PartitionSpec as P

MESH = pl.DeviceIdType.MESH
F32 = jnp.float32
BF16 = jnp.bfloat16

WX, WY, DZ, C = 2, 4, 48, 128
VOX = WX * WY * DZ
NZ = 8
NQ = 8
NXY = 2 * NQ
PAIRS = 14
ORDER = (4, 3, 5, 6, 7, 8, 0, 1, 2)
PRODUCTS = (((0, 1), (0, 1)), ((1, 3), (1, 2)), ((3, 5), (2, 4)), ((5, 7), (4, 5)), ((7, 9), (5, 7)))
CHUNKS = ((0, 2), (2, 4), (4, 7))
STEPS = ('c0', 'y', 'c1', 'm', 'c2', 'f0', 'p', 'c3', 'f1', 'c4', 'f2')


def slot(n, jz):
    return 3 * n + jz + (1 if n else 0)


XY = sorted(
    ((dx, dy) for dx in range(4) for dy in range(4) if dx or dy),
    key=lambda d: -(min(d[0], 4 - d[0]) + min(d[1], 4 - d[1])),
)
ZS = (4, 3, 5, 2, 6, 1, 7)
ROW = ((2, 0), (1, 0), (3, 0))
COLUMN = ((0, 2), (0, 1), (0, 3))
NEAR_Z = (2, 6, 1, 7)
DIRS = tuple((dx, dy) for dx in (-1, 1, 0) for dy in (-1, 0, 1) if (dx, dy) != (0, 0))


def blocks(w, local):
    jx, jy = w // 3, w % 3
    every = [(x, y) for x in range(WX) for y in range(WY)]
    inside = [(x, y) for x, y in every if 1 <= x + 2 - jx <= WX and 1 <= y + 2 - jy <= WY]
    return inside if local else [b for b in every if b not in inside]


LOCAL = [blocks(w, True) for w in range(9)]
RIM = [blocks(w, False) for w in range(9)]


def rim(d, width, send):
    if d == 0:
        return (1, width) if not send else (0, width)
    if send:
        return (width - 1, 1) if d > 0 else (0, 1)
    return (0, 1) if d > 0 else (width + 1, 1)


def body(
    inp_hbm, cot_hbm, ker_hbm, ig_ref, kg_ref,
    inp, wts, halo, stack, act, slope, acc, taps, parts, sib, xsend, xrecv, zsend, zrecv, sums,
    load_sem, hsend_sem, hrecv_sem, ssend_sem, srecv_sem, xsend_sem, xrecv_sem, zsend_sem, zrecv_sem,
    plane_in, z_in,
):
    gx, gy = lax.axis_index("gx"), lax.axis_index("gy")
    core, q = gy % 2, gy // 2
    z, yh = gx % NZ, gx // NZ
    here = yh * NQ + q
    px, py = q % 4, yh * 2 + q // 4
    other = gy + 1 - 2 * core

    def xy_peer(d):
        x, y = (px + d[0]) % 4, (py + d[1]) % 4
        m = y * 4 + x
        return m, ((m // NQ) * NZ + z, (m % NQ) * 2 + core)

    def z_peer(k):
        return (yh * NZ + k, gy)

    barrier = pltpu.get_barrier_semaphore()

    def greet(dev):
        pl.semaphore_signal(barrier, inc=1, device_id=dev, device_id_type=MESH)

    for dx, dy in DIRS:
        greet(((gx + dx + 16) % 16, (gy + dy + 16) % 16))
    for d in (*ROW, *COLUMN):
        greet(xy_peer(d)[1])
    for d in NEAR_Z:
        greet(z_peer((z + d) % NZ))

    own = halo.at[pl.ds(1, WX), pl.ds(1, WY)]
    load_cot = pltpu.make_async_copy(cot_hbm, own, load_sem.at[0])
    load_inp = pltpu.make_async_copy(inp_hbm, inp, load_sem.at[1])
    load_ker = pltpu.make_async_copy(ker_hbm, wts, load_sem.at[2])
    load_cot.start()
    load_inp.start()
    load_ker.start()

    def has(d, at, size):
        if d == 0:
            return 1
        return jnp.where(at < size - 1, 1, 0) if d > 0 else jnp.where(at > 0, 1, 0)

    def hop(i):
        dx, dy = DIRS[i]
        sx, sy = rim(dx, WX, True), rim(dy, WY, True)
        lx, ly = rim(dx, WX, False), rim(dy, WY, False)
        return pltpu.make_async_remote_copy(
            src_ref=halo.at[pl.ds(1 + sx[0], sx[1]), pl.ds(1 + sy[0], sy[1])],
            dst_ref=halo.at[pl.ds(*lx), pl.ds(*ly)],
            send_sem=hsend_sem.at[i],
            recv_sem=hrecv_sem.at[i],
            device_id=((gx + dx + 16) % 16, (gy + dy + 16) % 16),
            device_id_type=MESH,
        )

    load_cot.wait()
    pl.semaphore_wait(barrier, len(DIRS) + len(ROW) + len(COLUMN) + len(NEAR_Z))

    for i, (dx, dy) in enumerate(DIRS):
        @pl.when(has(dx, gx, 16) * has(dy, gy, 16) == 1)
        def _():
            hop(i).start()

    for d in ROW:
        pl.semaphore_signal(plane_in, inc=1, device_id=xy_peer(d)[1], device_id_type=MESH)
    for d in NEAR_Z:
        pl.semaphore_signal(z_in, inc=1, device_id=z_peer((z + d) % NZ), device_id_type=MESH)


    for i, (dx, dy) in enumerate(DIRS):
        lx, ly = rim(dx, WX, False), rim(dy, WY, False)

        @pl.when(has(-dx, gx, 16) * has(-dy, gy, 16) == 0)
        def _():
            halo[pl.ds(*lx), pl.ds(*ly)] = jnp.zeros((lx[1], ly[1], DZ, C), BF16)

    load_inp.wait()

    @pl.loop(0, WX)
    def _(x):
        v = inp[x].astype(F32).reshape(WY * DZ, C)
        cdf = 0.5 * (1.0 + lax.erf(v / math.sqrt(2.0)))
        slope[x] = cdf + v * jnp.exp(-0.5 * v * v) / math.sqrt(2.0 * math.pi)
        act[x] = (v * cdf).astype(BF16).astype(F32).reshape(WY, DZ, C)

    row = lax.broadcasted_iota(jnp.int32, (DZ, C), 0)

    def restack(x, y):
        v = halo[x, y].astype(F32)
        up = jnp.where(row == DZ - 1, 0.0, pltpu.roll(v, DZ - 1, 0))
        down = jnp.where(row == 0, 0.0, pltpu.roll(v, 1, 0))
        stack[x, y] = jnp.concatenate([up, v, down], axis=1).astype(BF16)


    @pl.loop(0, WX * WY)
    def _(k):
        restack(1 + k // WY, 1 + k % WY)

    def gather(lhs_blocks):
        return jnp.concatenate([act[x, y] for x, y in lhs_blocks], axis=0).T.astype(BF16)

    def product(w, chosen):
        jx, jy = w // 3, w % 3
        rows = [stack[x + 2 - jx, y + 2 - jy] for x, y in chosen]
        return jnp.dot(lhs[w, chosen is RIM[w]], jnp.concatenate(rows, axis=0), preferred_element_type=F32)

    lhs = {}
    for w in ORDER:
        lhs[w, False] = gather(LOCAL[w])
        if RIM[w]:
            lhs[w, True] = gather(RIM[w])
    for n, w in enumerate(ORDER):
        r = product(w, LOCAL[w])
        for jz in range(3):
            taps[slot(n, jz)] = r[:, jz * C : (jz + 1) * C]
    taps[3] = jnp.zeros((C, C), F32)
    def landed(along):
        for i, (dx, dy) in enumerate(DIRS):
            if dx != along:
                continue

            @pl.when(has(-dx, gx, 16) * has(-dy, gy, 16) == 1)
            def _():
                hop(i).wait_recv()

    def window(w):
        jx, jy = w // 3, w % 3
        return stack[pl.ds(2 - jx, WX), pl.ds(2 - jy, WY)].reshape(VOX, 3 * C)

    def sib_copy(v):
        return pltpu.make_async_remote_copy(
            src_ref=parts.at[1 - core, pl.ds(2 * v, 2)],
            dst_ref=sib.at[pl.ds(2 * v, 2)],
            send_sem=ssend_sem.at[v],
            recv_sem=srecv_sem.at[v],
            device_id=(gx, other),
            device_id_type=MESH,
        )

    def xy_copy(k, d):
        lo, hi = CHUNKS[k]
        m, twin = xy_peer(d)
        return pltpu.make_async_remote_copy(
            src_ref=xsend.at[m, pl.ds(lo, hi - lo)],
            dst_ref=xrecv.at[here, pl.ds(lo, hi - lo)],
            send_sem=xsend_sem.at[k],
            recv_sem=xrecv_sem.at[k],
            device_id=twin,
            device_id_type=MESH,
        )

    def xy_all(k):
        lo, hi = CHUNKS[k]
        return pltpu.make_async_remote_copy(
            src_ref=xsend.at[pl.ds(0, NXY - 1), pl.ds(lo, hi - lo)],
            dst_ref=xrecv.at[pl.ds(0, NXY - 1), pl.ds(lo, hi - lo)],
            send_sem=xsend_sem.at[k],
            recv_sem=xrecv_sem.at[k],
            device_id=(gx, other),
            device_id_type=MESH,
        )

    def z_copy(d):
        to = (z + d) % NZ
        return pltpu.make_async_remote_copy(
            src_ref=zsend.at[to],
            dst_ref=zrecv.at[z],
            send_sem=zsend_sem,
            recv_sem=zrecv_sem,
            device_id=z_peer(to),
            device_id_type=MESH,
        )

    z_all = pltpu.make_async_remote_copy(
        src_ref=zsend.at[pl.ds(0, NZ - 1)],
        dst_ref=zrecv.at[pl.ds(0, NZ - 1)],
        send_sem=zsend_sem,
        recv_sem=zrecv_sem,
        device_id=(gx, other),
        device_id_type=MESH,
    )

    def turn(v):
        for u in (2 * v, 2 * v + 1):
            for h in range(2):
                a = jnp.concatenate(
                    [taps[2 * u, 64 * h : 64 * h + 64], taps[2 * u + 1, 64 * h : 64 * h + 64]], axis=0
                )
                t = a.T.reshape(NQ, 2, 8, C)
                parts[0, u, h] = t[:, 0]
                parts[1, u, h] = t[:, 1]
        sib_copy(v).start()

    def compute(k):
        (w_lo, w_hi), (lo, hi) = PRODUCTS[k]
        done = lo
        for n in range(w_lo, w_hi):
            w = ORDER[n]
            if RIM[w]:
                r = product(w, RIM[w])
                for jz in range(3):
                    taps[slot(n, jz)] += r[:, jz * C : (jz + 1) * C]
            ready = min(hi, (slot(n, 2) + (2 if n == 0 else 1)) // 4)
            for v in range(done, ready):
                turn(v)
            done = max(done, ready)

    def forward(k):
        lo, hi = CHUNKS[k]
        for v in range(lo, hi):
            sib_copy(v).wait_recv()
            for h in range(2):
                both = [parts[core, 2 * v + e, h] + sib[2 * v + e, h] for e in range(2)]
                xsend[NQ * h : NQ * h + NQ, v] = jnp.concatenate(both, axis=1).astype(BF16)
        if k == 0:
            pl.semaphore_wait(plane_in, len(ROW))
        for d in XY:
            xy_copy(k, d).start()
        xrecv[here, lo:hi] = xsend[here, lo:hi]

    for step in STEPS:
        if step == "y":
            landed(0)
            for x in range(WX):
                restack(1 + x, 0)
                restack(1 + x, WY + 1)
        elif step == "m":
            landed(1)
            for y in range(WY + 2):
                restack(0, y)
        elif step == "p":
            landed(-1)
            for y in range(WY + 2):
                restack(WX + 1, y)
        elif step[0] == "c":
            compute(int(step[1]))
        else:
            forward(int(step[1]))

    load_ker.wait()
    acc[...] = jnp.zeros_like(acc)

    @pl.loop(0, 9)
    def _(w):
        wt = jnp.concatenate([wts[3 * w + jz] for jz in range(3)], axis=1)
        acc[...] += lax.dot_general(
            window(w), wt, (((1,), (1,)), ((), ())), preferred_element_type=F32
        )

    for x in range(WX):
        back = acc[pl.ds(x * WY * DZ, WY * DZ)]
        ig_ref[x] = (slope[x] * back).astype(BF16).reshape(WY, DZ, C)

    for k in range(len(CHUNKS)):
        lo, hi = CHUNKS[k]
        xy_all(k).wait_recv()
        total = xrecv[0, lo:hi].astype(F32)
        for m in range(1, NXY):
            total = total + xrecv[m, lo:hi].astype(F32)
        sums[pl.ds(16 * lo, 16 * (hi - lo))] = total.reshape(16 * (hi - lo), C)
    sums[pl.ds(8 * PAIRS, C - 8 * PAIRS)] = jnp.zeros((C - 8 * PAIRS, C), F32)
    total = jnp.concatenate([sums[pl.ds(o, 16, stride=8)] for o in range(8)], axis=0)
    turned = total.T.reshape(2, NZ, 8, C)
    for e in range(2):
        zsend[:, e] = turned[e]

    pl.semaphore_wait(z_in, len(NEAR_Z))
    for d in ZS:
        z_copy(d).start()
    zrecv[z] = zsend[z]

    for i, (dx, dy) in enumerate(DIRS):
        @pl.when(has(dx, gx, 16) * has(dy, gy, 16) == 1)
        def _():
            hop(i).wait_send()

    for k in range(len(CHUNKS)):
        xy_all(k).wait_send()
    for v in range(PAIRS // 2):
        sib_copy(v).wait_send()

    z_all.wait_recv()
    out = zrecv[0]
    for m in range(1, NZ):
        out = out + zrecv[m]
    kg_ref[...] = out
    z_all.wait_send()


def finish(ig_ref, sums_ref, out_ref, grad_ref, turn):
    out_ref[...] = ig_ref[...]
    total = sums_ref[...].reshape(16, C) / math.sqrt(32 * 64 * 48)
    for o in range(8):
        turn[pl.ds(o, 16, stride=8)] = pltpu.roll(total, (C - 16 * o) % C, 1)
    pair = turn[...].reshape(2, 8, 8, C)
    lane = lax.broadcasted_iota(jnp.int32, (8, C), 1)
    place = lane
    for n, w in enumerate(ORDER):
        place = jnp.where(lane // 3 == w, lane - 3 * w + slot(n, 0), place)
    source = jnp.minimum(place // 2, 15)
    for i in range(8):
        even = jnp.take_along_axis(pair[0, i], source, axis=1)
        odd = jnp.take_along_axis(pair[1, i], source, axis=1)
        grad_ref[i] = jnp.where(place % 2 == 0, even, odd)[:, :27]


def local(inputs, cotangent, kernel):
    n = len(CHUNKS)
    hbm = pl.BlockSpec(memory_space=pl.ANY)
    vmem = pl.BlockSpec(memory_space=pltpu.VMEM)
    dma = pltpu.SemaphoreType.DMA
    input_grad, sums = pl.pallas_call(
        body,
        out_shape=(
            jax.ShapeDtypeStruct((WX, WY, DZ, C), BF16),
            jax.ShapeDtypeStruct((2, 8, C), F32),
        ),
        in_specs=[hbm, hbm, hbm],
        out_specs=(vmem, vmem),
        scratch_shapes=[
            pltpu.VMEM((WX, WY, DZ, C), BF16),
            pltpu.VMEM((27, C, C), BF16),
            pltpu.VMEM((WX + 2, WY + 2, DZ, C), BF16),
            pltpu.VMEM((WX + 2, WY + 2, DZ, 3 * C), BF16),
            pltpu.VMEM((WX, WY, DZ, C), F32),
            pltpu.VMEM((WX, WY * DZ, C), F32),
            pltpu.VMEM((VOX, C), F32),
            pltpu.VMEM((28, C, C), F32),
            pltpu.VMEM((2, PAIRS, 2, NQ, 8, C), F32),
            pltpu.VMEM((PAIRS, 2, NQ, 8, C), F32),
            pltpu.VMEM((NXY, PAIRS // 2, 16, C), BF16),
            pltpu.VMEM((NXY, PAIRS // 2, 16, C), BF16),
            pltpu.VMEM((NZ, 2, 8, C), F32),
            pltpu.VMEM((NZ, 2, 8, C), F32),
            pltpu.VMEM((C, C), F32),
            dma((3,)),
            dma((8,)),
            dma((8,)),
            dma((PAIRS // 2,)),
            dma((PAIRS // 2,)),
            dma((n,)),
            dma((n,)),
            dma,
            dma,
            pltpu.SemaphoreType.REGULAR,
            pltpu.SemaphoreType.REGULAR,
        ],
        compiler_params=pltpu.CompilerParams(
            collective_id=0, has_side_effects=True, vmem_limit_bytes=32 * 1024 * 1024
        ),
        name="conv_backward",
    )(*(pltpu.with_memory_space_constraint(a, pltpu.HBM) for a in (inputs, cotangent, kernel)))
    whole = lambda shape: pl.BlockSpec(shape, lambda: (0,) * len(shape))
    input_grad, grad = pl.pallas_call(
        finish,
        out_shape=(
            jax.ShapeDtypeStruct((WX, WY, DZ, C), BF16),
            jax.ShapeDtypeStruct((8, 8, 27), F32),
        ),
        in_specs=[vmem, vmem],
        out_specs=(whole((WX, WY, DZ, C)), whole((8, 8, 27))),
        scratch_shapes=[pltpu.VMEM((C, C), F32)],
        compiler_params=pltpu.CompilerParams(vmem_limit_bytes=2 * 1024 * 1024),
        name="finish",
    )(input_grad, sums)
    return (input_grad, grad.transpose(2, 0, 1))


def solution(mesh):
    return jax.shard_map(
        local,
        mesh=mesh,
        in_specs=(P("gx", "gy", None, None), P("gx", "gy", None, None), P()),
        out_specs=(P("gx", "gy", None, None), P(None, "gx", "gy")),
        check_vma=False,
    )
```
